512 devices in a mesh: expert: 64 (over z, x_lo, core), hidden: 8 (over x_hi, y).
Axes of the slice: x: 4 (x_hi: 2, x_lo: 2; x = x_hi * 2 + x_lo), y: 4, z: 16, core: 2. Of those that a mesh axis runs over, the one named last changes fastest.
Arguments:
- swap_pairs: int32 [32, 2], replicated, may hold values from 0 to 63, as said below
- expert_ids: int32 [8192, 2], P('expert'), may hold values from 0 to 63, all different within a row; in each aligned block of 128 rows (0 to 127, 128 to 255, ...) at most 8 rows name the same one
- route_weights: float32 [8192, 2], P('expert'), may hold values from 0.05 to 0.6
- gate_up: bfloat16 [8192, 2, 2, 1024], P('expert', None, None, 'hidden'), may hold values from -6 to 6
- grad_out: bfloat16 [8192, 3584], P('expert', 'hidden'), may hold values from -6 to 6
- down_weight: bfloat16 [64, 1024, 3584], P('expert', 'hidden'), may hold values from -0.1875 to 0.1875
- first_moment: bfloat16 [64, 1024, 3584], P('expert', 'hidden'), may hold values from -4 to 4
- second_moment: bfloat16 [64, 1024, 3584], P('expert', 'hidden'), may hold values from 0.049804688 to 1
Outputs:
- combined: bfloat16 [8192, 3584], P('expert', 'hidden')
- grad_gate_up: bfloat16 [8192, 2, 2, 1024], P('expert', None, None, 'hidden')
- adam_step: bfloat16 [64, 1024, 3584], P('expert', 'hidden')
The draws below stay inside these ranges and needn't reach their ends.
Inputs may be any that keep to these rules, and one draw needn't show every extreme that they name: `swap_pairs`: every place 0 .. 63 appears exactly once in the list. `expert_ids`: A row's 2 experts are distinct; in each aligned block of 128 rows (the rows of one device) no expert is named more than 8 times, a bound that some block reaches.
All inputs are finite; a program needn't handle non-finite values.
Results may differ from the reference program's by a relative error of at most 0.017.
Values may be sent and summed in bfloat16 or wider, within the bound.
A program may use at most 128 MiB of HBM per device.

```python
import math
import jax
import jax.numpy as jnp
import numpy as np
from jax import lax

D = 3584
HID_DEV = 128
TOP = 2
TOK_DEV = 128
EXPERTS = 64
HID = 1024
TOKENS = 8192
CAP = 8
NSWAP = 32
N_HIDDEN = 8


def draw_swap_pairs(key, part):
    shuffled = jax.random.permutation(key, EXPERTS)
    return shuffled[:2 * NSWAP].reshape(NSWAP, 2).astype(jnp.int32)


def levels(rng, shape, cuts, low, largest):
    loudness, own = 1.0, jax.random.fold_in(rng, 6)
    for axis_at, parts in cuts:
        heights = jnp.exp(jax.random.uniform(jax.random.fold_in(own, axis_at), (parts,), jnp.float32, low / len(cuts), largest / len(cuts)))
        loudness = loudness * jnp.repeat(heights, shape[axis_at] // parts).reshape([-1 if axis == axis_at else 1 for axis in range(len(shape))])
    return loudness


def deal_out(own_key, own, number, rows, number_of, top, limit, slope):
    ranking = jax.random.permutation(own_key, number_of)
    packed, common = shares(number_of, rows * top, limit, slope, True), shares(number_of, rows * top, limit, slope, False)
    places = jnp.arange(number_of)

    def named(tallies, rotation):
        used = int((tallies > 0).sum())
        fixed = max(1, used // 4)
        moved = fixed + (places - fixed + rotation * (used - fixed)) % max(1, number_of - fixed)
        return jnp.zeros((number_of,), jnp.int32).at[ranking[jnp.where(places < fixed, places, moved)]].set(jnp.asarray(tallies, jnp.int32))

    tallies = jnp.where(number % 4 == 0, named(packed, number // 4), named(common, number - number // 4 - 1))
    mixed = jax.random.permutation(jax.random.fold_in(own, 3), number_of)
    giver, taker = mixed[0:number_of // 2 * 2:2], mixed[1:number_of // 2 * 2:2]
    margin = jnp.minimum(tallies[giver] - 1, limit - tallies[taker]) // 2
    margin = jnp.where((giver == ranking[0]) | (taker == ranking[0]) | (tallies[taker] == 0), 0, jnp.maximum(margin, 0))
    moved = jax.random.randint(jax.random.fold_in(own, 4), (number_of // 2,), 0, 1 << 20) % (margin + 1)
    tallies = tallies.at[giver].add(-moved).at[taker].add(moved)
    members = jnp.searchsorted(jnp.cumsum(tallies), jnp.arange(rows * top), side="right").astype(jnp.int32)
    grid = members.reshape(top, rows).T
    grid = grid[jax.random.permutation(jax.random.fold_in(own, 1), rows)]
    rotation = jax.random.randint(jax.random.fold_in(own, 2), (rows, 1), 0, top)
    return jnp.take_along_axis(grid, (jnp.arange(top)[None, :] + rotation) % top, axis=1)


def shares(amount, total, reach, lean, full):
    portions = [(1 << 20) // math.isqrt(rank ** lean) + 1 for rank in range(1, amount + 1)]
    largest = reach if full else min(reach, max(-(-total // amount), total * portions[0] // sum(portions)))
    least = 1 if total - largest >= amount - 1 else 0
    given, spare = [largest] + [least] * (amount - 1), total - largest - least * (amount - 1)
    while spare > 0:
        free = [i for i in range(1, amount) if given[i] < largest] or [i for i in range(1, amount) if given[i] < reach]
        pool, left = sum([portions[i] for i in free]), spare
        for i in free:
            more = min(reach - given[i], max(1, left * portions[i] // pool), spare)
            given[i] = given[i] + more
            spare = spare - more
    return np.array(given)


def noise(own_key, shape, scale, most, pieces=(), kind=jnp.bfloat16):
    level = levels(own_key, shape, pieces, -0.22, 0.18) if pieces else 1.0
    drawn = jax.random.normal(own_key, shape, jnp.float32) * scale * level
    return jnp.minimum(jnp.maximum(drawn, -most), most).astype(kind)


def setup_inputs(seed: int = 0) -> dict:
    keys = jax.random.split(jax.random.key(seed), 9)
    swap_pairs = draw_swap_pairs(jax.random.fold_in(keys[8], 71), 0)
    expert_ids_keys = jax.random.split(jax.random.fold_in(keys[1], 1), TOKENS // TOK_DEV)
    expert_ids_turns = jax.random.permutation(jax.random.fold_in(keys[1], 3), TOKENS // TOK_DEV)
    expert_ids = jax.vmap(lambda own, number: deal_out(jax.random.fold_in(keys[1], 2), own, number, TOK_DEV, EXPERTS, TOP, CAP, 2))(expert_ids_keys, expert_ids_turns).reshape((TOKENS, TOP))
    route_weights = jnp.clip(0.05 + 0.55 * jax.random.uniform(keys[2], (TOKENS, TOP), jnp.float32) ** levels(keys[2], (TOKENS, TOP), ((0, 64),), -0.2, 0.2), 0.05, 0.6)
    gate_up = noise(keys[3], (TOKENS, TOP, 2, HID), 1.0, 6.0, ((0, 64), (3, 8)))
    grad_out = noise(keys[4], (TOKENS, D), 1.0, 6.0, ((0, 64), (1, 8)))
    down_weight = noise(keys[5], (EXPERTS, HID, D), HID ** -0.5, 0.1875, ((0, 64), (1, 8)))
    first_moment = noise(keys[6], (EXPERTS, HID, D), 0.5, 4.0, ((0, 64), (1, 8)))
    second_moment = jnp.clip(jnp.exp(math.log(1.0) - 2.9996462 * jax.random.uniform(keys[7], (EXPERTS, HID, D), jnp.float32) ** levels(keys[7], (EXPERTS, HID, D), ((0, 64), (1, 8)), -0.2, 0.2)), 0.049804688, 1.0).astype(jnp.bfloat16)
    return {"swap_pairs": swap_pairs, "expert_ids": expert_ids, "route_weights": route_weights, "gate_up": gate_up, "grad_out": grad_out, "down_weight": down_weight, "first_moment": first_moment, "second_moment": second_moment}


first_decay = 0.9
second_decay = 0.95
adam_epsilon = 1e-08

def partner_table(swap_pairs, places):
    column = jnp.arange(places, dtype=jnp.int32)
    left = swap_pairs[:, 0].astype(jnp.int32)
    right = swap_pairs[:, 1].astype(jnp.int32)
    moved = jnp.where(left[:, None] == column[None, :], right[:, None] - column[None, :], 0)
    moved = moved + jnp.where(right[:, None] == column[None, :], left[:, None] - column[None, :], 0)
    return (column + lax.optimization_barrier(jnp.sum(moved, axis=0))).astype(jnp.int32)

def reference(swap_pairs, expert_ids, route_weights, gate_up, grad_out, down_weight, first_moment, second_moment):
    partner = partner_table(swap_pairs, EXPERTS)
    flat_ids = expert_ids.reshape(-1).astype(jnp.int32)
    choices = flat_ids.shape[0]
    sorted_order = jnp.argsort(flat_ids, stable=True).astype(jnp.int32)
    column = jnp.arange(EXPERTS, dtype=jnp.int32)
    counts = lax.optimization_barrier(jnp.sum((flat_ids[:, None] == column[None, :]).astype(jnp.int32), axis=0))
    starts = (jnp.cumsum(counts) - counts).astype(jnp.int32)
    slot_limit = EXPERTS * CAP
    lane_index = jnp.arange(slot_limit, dtype=jnp.int32)
    act_table = gate_up.reshape(choices, 2 * HID)
    weight_flat = route_weights.reshape(-1)

    def one_expert(totals, expert):
        mixed_total, grad_total = totals
        is_valid = lane_index < counts[expert]
        picked = jnp.take(sorted_order, jnp.where(is_valid, starts[expert] + lane_index, 0).astype(jnp.int32)).astype(jnp.int32)
        token_row = (picked // TOP).astype(jnp.int32)
        act_pick = jnp.where(is_valid[:, None], jnp.take(act_table, picked, axis=0), jnp.zeros((), act_table.dtype))
        gate_pre = act_pick[:, :HID].astype(jnp.float32)
        up_pre = act_pick[:, HID:].astype(jnp.float32)
        sigmoid_gate = jax.nn.sigmoid(gate_pre)
        silu_gate = gate_pre * sigmoid_gate
        hidden = (silu_gate * up_pre).astype(jnp.bfloat16)
        factor = jnp.where(is_valid, jnp.take(weight_flat, picked), jnp.zeros((), jnp.float32))
        scaled = (factor[:, None] * jnp.take(grad_out, token_row, axis=0).astype(jnp.float32)).astype(jnp.bfloat16)
        weight = lax.dynamic_index_in_dim(down_weight, expert, 0, keepdims=False)
        grouped = jnp.einsum('rjh,jhd->jrd', hidden.reshape(slot_limit, N_HIDDEN, HID_DEV).astype(jnp.float32), weight.reshape(N_HIDDEN, HID_DEV, D).astype(jnp.float32))
        grouped = lax.optimization_barrier(grouped.astype(jnp.bfloat16))
        summed = lax.optimization_barrier(jnp.sum(grouped.astype(jnp.float32), axis=0))
        mixed_total = mixed_total.at[token_row].add(factor[:, None] * summed)
        grad_hidden = jnp.dot(scaled, weight.T, preferred_element_type=jnp.float32)
        grad_gate = grad_hidden * up_pre * sigmoid_gate * (1.0 + gate_pre * (1.0 - sigmoid_gate))
        grad_up = grad_hidden * silu_gate
        grad_rows = jnp.concatenate([grad_gate, grad_up], axis=1).astype(jnp.bfloat16)
        grad_rows = jnp.where(is_valid[:, None], grad_rows, jnp.zeros((), grad_rows.dtype))
        grad_total = grad_total.at[picked].add(grad_rows)
        grad_weight = jnp.dot(hidden.T, scaled, preferred_element_type=jnp.float32)
        first_here = lax.dynamic_index_in_dim(first_moment, expert, 0, keepdims=False).astype(jnp.float32)
        second_here = lax.dynamic_index_in_dim(second_moment, expert, 0, keepdims=False).astype(jnp.float32)
        first_new = first_decay * first_here + (1.0 - first_decay) * grad_weight
        second_new = second_decay * second_here + (1.0 - second_decay) * grad_weight * grad_weight
        update = (first_new / (jnp.sqrt(second_new) + adam_epsilon)).astype(jnp.bfloat16)
        return ((mixed_total, grad_total), update)
    initial = (jnp.zeros((TOKENS, D), jnp.float32), jnp.zeros((choices, 2 * HID), jnp.bfloat16))
    totals, updates = lax.scan(one_expert, initial, jnp.arange(EXPERTS, dtype=jnp.int32))
    combined = totals[0].astype(jnp.bfloat16)
    grad_gate_up = totals[1].reshape(TOKENS, TOP, 2, HID)
    adam_step = jnp.take(updates, partner, axis=0)
    return (combined, grad_gate_up, adam_step)
```

```python
import functools

import jax
import jax.numpy as jnp
from jax import lax
from jax.experimental import pallas as pl
from jax.experimental.pallas import tpu as pltpu
from jax.sharding import PartitionSpec as P

first_decay = 0.9
second_decay = 0.95
adam_epsilon = 1e-08
ROWS = 16
COLS = 512


def partner_table(swap_pairs, places):
    column = jnp.arange(places, dtype=jnp.int32)
    left = swap_pairs[:, 0]
    right = swap_pairs[:, 1]
    moved = jnp.where(left[:, None] == column[None, :], right[:, None] - column[None, :], 0)
    moved = moved + jnp.where(right[:, None] == column[None, :], left[:, None] - column[None, :], 0)
    return column + jnp.sum(moved, axis=0)


def dot(a, b, contract_a, contract_b):
    return lax.dot_general(
        a, b, (((contract_a,), (contract_b,)), ((), ())), preferred_element_type=jnp.float32
    )


def kernel(
    places,
    n_hidden,
    capacity,
    partner_ref,
    ids_ref,
    route_ref,
    acts_ref,
    gout_ref,
    w_hbm,
    m_hbm,
    v_hbm,
    comb_ref,
    ggu_ref,
    upd_hbm,
    w_here,
    m_here,
    v_here,
    table,
    h_send,
    h_recv,
    g_send,
    g_recv,
    w_send,
    w_recv,
    h_own,
    h_all,
    y_send,
    y_recv,
    gw_send,
    gw_recv,
    gh_send,
    gh_recv,
    gr_send,
    gr_recv,
    u_here,
    u_mid,
    u_out,
    u_new,
    local_sem,
    send_sem,
    recv_sem,
):
    me = lax.axis_index("expert")
    mine = lax.axis_index("hidden")
    tok = ids_ref.shape[0]
    slots = places * capacity
    unit = h_own.shape[1]
    feat = gout_ref.shape[1]
    col_groups = w_here.shape[1] // COLS
    row_groups = w_here.shape[0] // ROWS
    stride = places // row_groups

    def expert_peer(step):
        half = (step + 1) // 2
        return lax.rem(me + half + (1 - lax.rem(step, 2)) * (places - 2 * half), places)

    def hidden_peer(step):
        return lax.rem(mine + step, n_hidden)

    barrier = pltpu.get_barrier_semaphore()

    def greet_expert(step, carry):
        pl.semaphore_signal(barrier, inc=1, device_id={"expert": lax.rem(me + step, places)})
        return carry

    def greet_hidden(step, carry):
        pl.semaphore_signal(barrier, inc=1, device_id={"hidden": hidden_peer(step)})
        return carry

    lax.fori_loop(1, places, greet_expert, 0)
    lax.fori_loop(1, n_hidden, greet_hidden, 0)

    loads = [
        pltpu.make_async_copy(src, dst, local_sem.at[at])
        for at, (src, dst) in enumerate(((w_hbm, w_here), (m_hbm, m_here), (v_hbm, v_here)))
    ]
    for load in loads:
        load.start()

    ids = jnp.concatenate([ids_ref[:, 0:1], ids_ref[:, 1:2]], axis=0)
    count = 2 * tok
    hot = (ids == lax.broadcasted_iota(jnp.int32, (count, 128), 1)).astype(jnp.float32)
    earlier = (
        lax.broadcasted_iota(jnp.int32, (count, count), 1)
        < lax.broadcasted_iota(jnp.int32, (count, count), 0)
    ).astype(jnp.bfloat16)
    before = dot(earlier, hot.astype(jnp.bfloat16), 1, 0)
    rank = jnp.sum(before * hot, axis=1, keepdims=True).astype(jnp.int32)
    slot = ids * capacity + rank
    table[...] = (slot == lax.broadcasted_iota(jnp.int32, (count, slots), 1)).astype(jnp.bfloat16)

    def gate_and_up(choice):
        at = choice * 2 * unit
        gate = acts_ref[:, at : at + unit].astype(jnp.float32)
        up = acts_ref[:, at + unit : at + 2 * unit].astype(jnp.float32)
        return gate, up

    rows = []
    for choice in range(2):
        gate, up = gate_and_up(choice)
        rows.append((gate * jax.nn.sigmoid(gate) * up).astype(jnp.bfloat16))
    placed = dot(table[...], jnp.concatenate(rows, axis=0), 0, 0)
    h_send[...] = placed.reshape(places, capacity, unit).astype(jnp.bfloat16)

    def to_experts(src, dst, at):
        def send(step, carry):
            peer = expert_peer(step)
            pltpu.make_async_remote_copy(
                src_ref=src.at[peer],
                dst_ref=dst.at[me],
                send_sem=send_sem.at[at],
                recv_sem=recv_sem.at[at],
                device_id={"expert": peer},
            ).start()
            return carry

        lax.fori_loop(1, places, send, 0)
        pltpu.make_async_copy(src.at[me], dst.at[me], recv_sem.at[at]).start()

    def to_hidden(src, dst, at, block=True):
        def send(step, carry):
            peer = hidden_peer(step)
            pltpu.make_async_remote_copy(
                src_ref=src.at[peer] if block else src,
                dst_ref=dst.at[mine],
                send_sem=send_sem.at[at],
                recv_sem=recv_sem.at[at],
                device_id={"hidden": peer},
            ).start()
            return carry

        lax.fori_loop(1, n_hidden, send, 0)
        pltpu.make_async_copy(
            src.at[mine] if block else src, dst.at[mine], recv_sem.at[at]
        ).start()

    def arrived(dst, at):
        pltpu.make_async_copy(dst, dst, recv_sem.at[at]).wait()

    def sent(src, at):
        pltpu.make_async_copy(src, src, send_sem.at[at]).wait()

    pl.semaphore_wait(barrier, places + n_hidden - 2)
    to_experts(h_send, h_recv, 0)

    loads[0].wait()
    for block in range(n_hidden):
        w_send[block] = w_here[:, block * feat : (block + 1) * feat]
    to_hidden(w_send, w_recv, 1)

    rows = [
        (route_ref[:, choice : choice + 1] * gout_ref[...].astype(jnp.float32)).astype(jnp.bfloat16)
        for choice in range(2)
    ]
    placed = dot(table[...], jnp.concatenate(rows, axis=0), 0, 0)
    g_send[...] = placed.reshape(places, capacity, feat).astype(jnp.bfloat16)
    to_experts(g_send, g_recv, 2)

    arrived(h_recv, 0)
    h_own[...] = h_recv[...].astype(jnp.float32).reshape(slots, unit).astype(jnp.bfloat16)
    to_hidden(h_own, h_all, 3, block=False)

    arrived(h_all, 3)
    arrived(w_recv, 1)
    w_all = w_recv[...].reshape(n_hidden * unit, feat)
    h_cat = jnp.concatenate([h_all[block] for block in range(n_hidden)], axis=1)
    y_send[...] = dot(h_cat, w_all, 1, 0).reshape(places, capacity, feat).astype(jnp.bfloat16)
    to_experts(y_send, y_recv, 4)

    arrived(g_recv, 2)
    grads = g_recv[...].astype(jnp.float32).reshape(slots, feat).astype(jnp.bfloat16)
    for block in range(n_hidden):
        gw_send[block] = dot(h_all[block], grads, 0, 0).astype(jnp.bfloat16)
    to_hidden(gw_send, gw_recv, 5)
    for block in range(n_hidden):
        gh_send[block] = dot(grads, w_recv[block], 1, 1).astype(jnp.bfloat16)
    to_hidden(gh_send, gh_recv, 6)

    arrived(gw_recv, 5)
    loads[1].wait()
    loads[2].wait()
    is_mid = lax.rem(me, stride) < col_groups
    my_row = pl.multiple_of((me // stride) * ROWS, ROWS)
    my_col = pl.multiple_of(lax.rem(me, stride) * COLS, COLS)

    def update_rows(step, carry):
        half = (step + 1) // 2
        group = lax.rem(
            me // stride + half + (1 - lax.rem(step, 2)) * (row_groups - 2 * half), row_groups
        )
        at = pl.multiple_of(group * ROWS, ROWS)
        for pair in range(n_hidden // 2):
            span = slice(pair * 2 * feat, (pair + 1) * 2 * feat)
            grad = jnp.concatenate(
                [
                    gw_recv[2 * pair, pl.ds(at, ROWS), :],
                    gw_recv[2 * pair + 1, pl.ds(at, ROWS), :],
                ],
                axis=1,
            ).astype(jnp.float32)
            first = m_here[pl.ds(at, ROWS), span].astype(jnp.float32)
            second = v_here[pl.ds(at, ROWS), span].astype(jnp.float32)
            first_new = first_decay * first + (1.0 - first_decay) * grad
            second_new = second_decay * second + (1.0 - second_decay) * grad * grad
            u_here[pl.ds(at, ROWS), span] = (
                first_new / (jnp.sqrt(second_new) + adam_epsilon)
            ).astype(jnp.bfloat16)

        def send(col, carry):
            peer = group * stride + col
            chunk = u_here.at[pl.ds(at, ROWS), pl.ds(pl.multiple_of(col * COLS, COLS), COLS)]

            @pl.when(peer == me)
            def _():
                pltpu.make_async_copy(chunk, u_mid.at[me], recv_sem.at[7]).start()

            @pl.when(peer != me)
            def _():
                pltpu.make_async_remote_copy(
                    src_ref=chunk,
                    dst_ref=u_mid.at[me],
                    send_sem=send_sem.at[7],
                    recv_sem=recv_sem.at[7],
                    device_id={"expert": peer},
                ).start()

            return carry

        return lax.fori_loop(0, col_groups, send, carry)

    lax.fori_loop(0, row_groups, update_rows, 0)

    arrived(gh_recv, 6)
    total = gh_recv[0].astype(jnp.float32)
    for block in range(1, n_hidden):
        total = total + gh_recv[block].astype(jnp.float32)
    gr_send[...] = total.reshape(places, capacity, unit).astype(jnp.bfloat16)
    to_experts(gr_send, gr_recv, 8)

    arrived(y_recv, 4)
    back = y_recv[...].astype(jnp.float32).reshape(slots, feat).astype(jnp.bfloat16)
    picked = dot(table[...], back, 1, 0)
    comb_ref[...] = (
        route_ref[:, 0:1] * picked[:tok] + route_ref[:, 1:2] * picked[tok:]
    ).astype(jnp.bfloat16)

    @pl.when(is_mid)
    def _():
        arrived(u_mid, 7)

        def forward(step, carry):
            peer = expert_peer(step)
            u_out[peer] = u_mid[partner_ref[peer]]
            pltpu.make_async_remote_copy(
                src_ref=u_out.at[peer],
                dst_ref=u_new.at[pl.ds(my_row, ROWS), pl.ds(my_col, COLS)],
                send_sem=send_sem.at[9],
                recv_sem=recv_sem.at[9],
                device_id={"expert": peer},
            ).start()
            return carry

        lax.fori_loop(1, places, forward, 0)
        u_out[me] = u_mid[partner_ref[me]]
        pltpu.make_async_copy(
            u_out.at[me], u_new.at[pl.ds(my_row, ROWS), pl.ds(my_col, COLS)], recv_sem.at[9]
        ).start()

    arrived(gr_recv, 8)
    back = gr_recv[...].astype(jnp.float32).reshape(slots, unit).astype(jnp.bfloat16)
    picked = dot(table[...], back, 1, 0)
    for choice in range(2):
        gate, up = gate_and_up(choice)
        sig = jax.nn.sigmoid(gate)
        grad_hidden = picked[choice * tok : (choice + 1) * tok]
        at = choice * 2 * unit
        ggu_ref[:, at : at + unit] = (
            grad_hidden * up * sig * (1.0 + gate * (1.0 - sig))
        ).astype(jnp.bfloat16)
        ggu_ref[:, at + unit : at + 2 * unit] = (grad_hidden * (gate * sig)).astype(jnp.bfloat16)

    arrived(u_new, 9)
    store = pltpu.make_async_copy(u_new, upd_hbm, local_sem.at[0])
    store.start()
    for at, src in ((0, h_send), (2, g_send), (4, y_send), (8, gr_send)):
        sent(src.at[pl.ds(0, places - 1)], at)
    for at, src in ((1, w_send), (3, h_all), (5, gw_send), (6, gh_send)):
        sent(src.at[pl.ds(0, n_hidden - 1)], at)

    @pl.when(is_mid)
    def _():
        sent(u_mid.at[pl.ds(0, row_groups * col_groups - 1)], 7)
        sent(u_out.at[pl.ds(0, places - 1)], 9)

    @pl.when(jnp.logical_not(is_mid))
    def _():
        sent(u_mid.at[pl.ds(0, row_groups * col_groups)], 7)

    store.wait()


def local(
    swap_pairs,
    expert_ids,
    route_weights,
    gate_up,
    grad_out,
    down_weight,
    first_moment,
    second_moment,
):
    places = lax.axis_size("expert")
    n_hidden = lax.axis_size("hidden")
    tok, top = expert_ids.shape
    unit, depth = down_weight.shape[1:]
    feat = grad_out.shape[1]
    capacity = 2 * tok * top // places
    slots = places * capacity
    partner = partner_table(swap_pairs, places)
    bf16 = jnp.bfloat16
    vmem = pl.BlockSpec(memory_space=pltpu.VMEM)
    anywhere = pl.BlockSpec(memory_space=pl.ANY)
    scratch = [
        ((unit, depth), bf16),
        ((unit, depth), bf16),
        ((unit, depth), bf16),
        ((tok * top, slots), bf16),
        ((places, capacity, unit), bf16),
        ((places, capacity, unit), bf16),
        ((places, capacity, feat), bf16),
        ((places, capacity, feat), bf16),
        ((n_hidden, unit, feat), bf16),
        ((n_hidden, unit, feat), bf16),
        ((slots, unit), bf16),
        ((n_hidden, slots, unit), bf16),
        ((places, capacity, feat), bf16),
        ((places, capacity, feat), bf16),
        ((n_hidden, unit, feat), bf16),
        ((n_hidden, unit, feat), bf16),
        ((n_hidden, slots, unit), bf16),
        ((n_hidden, slots, unit), bf16),
        ((places, capacity, unit), bf16),
        ((places, capacity, unit), bf16),
        ((unit, depth), bf16),
        ((places, ROWS, COLS), bf16),
        ((places, ROWS, COLS), bf16),
        ((unit, depth), bf16),
    ]
    combined, grads, update = pl.pallas_call(
        functools.partial(kernel, places, n_hidden, capacity),
        out_shape=(
            jax.ShapeDtypeStruct((tok, feat), bf16),
            jax.ShapeDtypeStruct((tok, top * 2 * unit), bf16),
            jax.ShapeDtypeStruct((unit, depth), bf16),
        ),
        in_specs=[pl.BlockSpec(memory_space=pltpu.SMEM)] + [vmem] * 4 + [anywhere] * 3,
        out_specs=(vmem, vmem, anywhere),
        scratch_shapes=[pltpu.VMEM(shape, kind) for shape, kind in scratch]
        + [
            pltpu.SemaphoreType.DMA((3,)),
            pltpu.SemaphoreType.DMA((10,)),
            pltpu.SemaphoreType.DMA((10,)),
        ],
        compiler_params=pltpu.CompilerParams(
            collective_id=0, has_side_effects=True, vmem_limit_bytes=48 * 1024 * 1024
        ),
    )(
        partner,
        expert_ids,
        route_weights,
        gate_up.reshape(tok, top * 2 * unit),
        grad_out,
        down_weight[0],
        first_moment[0],
        second_moment[0],
    )
    return combined, grads.reshape(tok, top, 2, unit), update[None]


def solution(mesh):
    placed = (
        P(),
        P("expert", None),
        P("expert", None),
        P("expert", None, None, "hidden"),
        P("expert", "hidden"),
        P("expert", "hidden", None),
        P("expert", "hidden", None),
        P("expert", "hidden", None),
    )
    return jax.shard_map(
        local,
        mesh=mesh,
        in_specs=placed,
        out_specs=(
            P("expert", "hidden"),
            P("expert", None, None, "hidden"),
            P("expert", "hidden", None),
        ),
        check_vma=False,
    )
```

```python
import functools

import jax
import jax.numpy as jnp
from jax import lax
from jax.experimental import pallas as pl
from jax.experimental.pallas import tpu as pltpu
from jax.sharding import PartitionSpec as P

first_decay = 0.9
second_decay = 0.95
adam_epsilon = 1e-08
ROWS = 16
COLS = 512
PARTS = 1
VMEM_BYTES = 60 * 1024 * 1024


def dot(a, b, contract_a, contract_b):
    return lax.dot_general(
        a, b, (((contract_a,), (contract_b,)), ((), ())), preferred_element_type=jnp.float32
    )


def kernel(
    places,
    n_hidden,
    capacity,
    swap_ref,
    ids_ref,
    route_ref,
    acts_ref,
    gout_ref,
    w_hbm,
    m_hbm,
    v_hbm,
    comb_ref,
    ggu_ref,
    upd_hbm,
    w_here,
    m_here,
    v_here,
    table,
    h_send,
    h_recv,
    g_send,
    g_recv,
    w_send,
    w_recv,
    h_own,
    h_all,
    y_send,
    y_recv,
    gw_send,
    gw_recv,
    gh_send,
    gh_recv,
    gr_send,
    gr_recv,
    u_here,
    u_mid,
    u_out,
    partner_row,
    partner_ref,
    local_sem,
    send_sem,
    recv_sem,
):
    me = lax.axis_index("expert")
    mine = lax.axis_index("hidden")
    tok = ids_ref.shape[1]
    count = 2 * tok
    slots = places * capacity
    unit = h_own.shape[1]
    feat = gout_ref.shape[0]
    row_groups = w_here.shape[0] // ROWS
    col_groups = w_here.shape[1] // COLS
    stride = places // row_groups

    def far_first(at, step, length):
        near = length - step
        half = (near + 1) // 2
        return lax.rem(at + half + (1 - lax.rem(near, 2)) * (length - 2 * half), length)

    def expert_peer(step):
        return far_first(me, step, places)

    def hidden_peer(step):
        return lax.rem(mine + step, n_hidden)

    barrier = pltpu.get_barrier_semaphore()

    def greet_expert(step, carry):
        pl.semaphore_signal(barrier, inc=1, device_id={"expert": expert_peer(step)})
        return carry

    def greet_hidden(step, carry):
        pl.semaphore_signal(barrier, inc=1, device_id={"hidden": hidden_peer(step)})
        return carry

    lax.fori_loop(1, places, greet_expert, 0)
    lax.fori_loop(1, n_hidden, greet_hidden, 0)

    loads = [
        pltpu.make_async_copy(src, dst, local_sem.at[at])
        for at, (src, dst) in enumerate(((w_hbm, w_here), (m_hbm, m_here), (v_hbm, v_here)))
    ]
    for load in loads:
        load.start()

    ids = jnp.concatenate([ids_ref[0:1, :], ids_ref[1:2, :]], axis=1)
    hot = (lax.broadcasted_iota(jnp.int32, (places, count), 0) == ids).astype(jnp.float32)
    earlier = (
        lax.broadcasted_iota(jnp.int32, (count, count), 0)
        < lax.broadcasted_iota(jnp.int32, (count, count), 1)
    ).astype(jnp.bfloat16)
    before = dot(hot.astype(jnp.bfloat16), earlier, 1, 0)
    rank = jnp.sum(before * hot, axis=0, keepdims=True).astype(jnp.int32)
    slot = ids * capacity + rank
    table[...] = (lax.broadcasted_iota(jnp.int32, (slots, count), 0) == slot).astype(jnp.bfloat16)

    def gate_and_up(choice):
        at = choice * 2 * unit
        gate = acts_ref[:, at : at + unit].astype(jnp.float32)
        up = acts_ref[:, at + unit : at + 2 * unit].astype(jnp.float32)
        return gate, up

    rows = []
    for choice in range(2):
        gate, up = gate_and_up(choice)
        rows.append((gate * jax.nn.sigmoid(gate) * up).astype(jnp.bfloat16))
    placed = dot(table[...], jnp.concatenate(rows, axis=0), 1, 0)
    h_send[...] = placed.reshape(places, capacity, unit).astype(jnp.bfloat16)

    unsent = []

    def arrived(dst, at):
        pltpu.make_async_copy(dst, dst, recv_sem.at[at]).wait()

    def sent(src, at):
        pltpu.make_async_copy(src, src, send_sem.at[at]).wait()

    def to_experts(src, dst, at, first=1, last=places):
        def send(step, carry):
            peer = expert_peer(step)
            pltpu.make_async_remote_copy(
                src_ref=src.at[peer],
                dst_ref=dst.at[me],
                send_sem=send_sem.at[at],
                recv_sem=recv_sem.at[at],
                device_id={"expert": peer},
            ).start()
            return carry

        lax.fori_loop(first, last, send, 0)
        if last == places:
            pltpu.make_async_copy(src.at[me], dst.at[me], recv_sem.at[at]).start()
            unsent.append((dst.at[pl.ds(0, places - 1)], at))

    def to_hidden(src, dst, at, block=True):
        def send(step, carry):
            peer = hidden_peer(step)
            pltpu.make_async_remote_copy(
                src_ref=src.at[peer] if block else src,
                dst_ref=dst.at[mine],
                send_sem=send_sem.at[at],
                recv_sem=recv_sem.at[at],
                device_id={"hidden": peer},
            ).start()
            return carry

        lax.fori_loop(1, n_hidden, send, 0)
        pltpu.make_async_copy(
            src.at[mine] if block else src, dst.at[mine], recv_sem.at[at]
        ).start()
        unsent.append((dst.at[pl.ds(0, n_hidden - 1)], at))

    rows = [
        (route_ref[choice : choice + 1, :] * gout_ref[...].astype(jnp.float32)).astype(jnp.bfloat16)
        for choice in range(2)
    ]
    placed = dot(table[...], jnp.concatenate(rows, axis=1), 1, 1)
    g_send[...] = placed.reshape(places, capacity, feat).astype(jnp.bfloat16)
    loads[0].wait()
    for block in range(n_hidden):
        w_send[block] = w_here[:, block * feat : (block + 1) * feat]

    def send_blocks(product, src, dst, at):
        def send(step, carry):
            peer = hidden_peer(step)
            src[peer] = product(peer).astype(jnp.bfloat16)
            pltpu.make_async_remote_copy(
                src_ref=src.at[peer],
                dst_ref=dst.at[mine],
                send_sem=send_sem.at[at],
                recv_sem=recv_sem.at[at],
                device_id={"hidden": peer},
            ).start()
            return carry

        lax.fori_loop(1, n_hidden, send, 0)
        src[mine] = product(mine).astype(jnp.bfloat16)
        pltpu.make_async_copy(src.at[mine], dst.at[mine], recv_sem.at[at]).start()
        unsent.append((dst.at[pl.ds(0, n_hidden - 1)], at))

    pl.semaphore_wait(barrier, places + n_hidden - 2)
    to_hidden(w_send, w_recv, 1)
    to_experts(h_send, h_recv, 0)
    to_experts(g_send, g_recv, 2)

    place = lax.broadcasted_iota(jnp.int32, (128, swap_ref.shape[1]), 0)
    left, right = swap_ref[0:1, :], swap_ref[1:2, :]
    trades = jnp.where(place == left, right, 0) + jnp.where(place == right, left, 0)
    trades = jnp.sum(trades, axis=1, keepdims=True)
    partner_row[...] = jnp.broadcast_to(trades, (128, 128)).T[0:1, :]
    table_copy = pltpu.make_async_copy(partner_row, partner_ref, local_sem.at[3])
    table_copy.start()

    arrived(h_recv, 0)
    h_own[...] = h_recv[...].astype(jnp.float32).reshape(slots, unit).astype(jnp.bfloat16)
    to_hidden(h_own, h_all, 3, block=False)
    arrived(w_recv, 1)
    arrived(h_all, 3)
    w_all = w_recv[...].reshape(n_hidden * unit, feat)
    h_cat = jnp.concatenate([h_all[block] for block in range(n_hidden)], axis=1)
    y_send[...] = dot(h_cat, w_all, 1, 0).reshape(places, capacity, feat).astype(jnp.bfloat16)
    to_experts(y_send, y_recv, 4, 1, places // 2)
    arrived(g_recv, 2)
    grads = g_recv[...].astype(jnp.float32).reshape(slots, feat).astype(jnp.bfloat16)
    send_blocks(lambda block: dot(h_all[block], grads, 0, 0), gw_send, gw_recv, 5)
    to_experts(y_send, y_recv, 4, places // 2, places)

    arrived(gw_recv, 5)
    loads[1].wait()
    loads[2].wait()
    is_mid = lax.rem(me, stride) < col_groups
    my_row = pl.multiple_of((me // stride) * ROWS, ROWS)
    my_col = lax.rem(me, stride) * COLS
    wide = COLS // PARTS

    def column_at(base, part):
        return pl.ds(pl.multiple_of(base + part * wide, wide), wide)

    def send_rows(group, part):
        at = pl.multiple_of(group * ROWS, ROWS)

        def send(col, carry):
            peer = group * stride + col
            chunk = u_here.at[pl.ds(at, ROWS), column_at(col * COLS, part)]

            @pl.when(peer == me)
            def _():
                pltpu.make_async_copy(chunk, u_mid.at[part, me], recv_sem.at[8 + part]).start()

            @pl.when(peer != me)
            def _():
                pltpu.make_async_remote_copy(
                    src_ref=chunk,
                    dst_ref=u_mid.at[part, me],
                    send_sem=send_sem.at[8 + part],
                    recv_sem=recv_sem.at[8 + part],
                    device_id={"expert": peer},
                ).start()

            return carry

        lax.fori_loop(0, col_groups, send, 0)

    def row_group(step):
        return far_first(me // stride, step, row_groups)

    def update_rows(step, carry):
        group = row_group(step)
        at = pl.multiple_of(group * ROWS, ROWS)
        for pair in range(n_hidden // 2):
            span = slice(pair * 2 * feat, (pair + 1) * 2 * feat)
            grad = jnp.concatenate(
                [
                    gw_recv[2 * pair, pl.ds(at, ROWS), :],
                    gw_recv[2 * pair + 1, pl.ds(at, ROWS), :],
                ],
                axis=1,
            ).astype(jnp.float32)
            first = m_here[pl.ds(at, ROWS), span].astype(jnp.float32)
            second = v_here[pl.ds(at, ROWS), span].astype(jnp.float32)
            first_new = first_decay * first + (1.0 - first_decay) * grad
            second_new = second_decay * second + (1.0 - second_decay) * grad * grad
            u_here[pl.ds(at, ROWS), span] = (
                first_new / (jnp.sqrt(second_new) + adam_epsilon)
            ).astype(jnp.bfloat16)
        send_rows(group, 0)
        return carry

    lax.fori_loop(1, row_groups + 1, update_rows, 0)
    send_blocks(lambda block: dot(grads, w_recv[block], 1, 1), gh_send, gh_recv, 6)

    arrived(y_recv, 4)
    back = y_recv[...].astype(jnp.float32).reshape(slots, feat).astype(jnp.bfloat16)
    picked = dot(back, table[...], 0, 0)
    comb_ref[...] = (
        route_ref[0:1, :] * picked[:, :tok] + route_ref[1:2, :] * picked[:, tok:]
    ).astype(jnp.bfloat16)
    arrived(gh_recv, 6)
    total = gh_recv[0].astype(jnp.float32)
    for block in range(1, n_hidden):
        total = total + gh_recv[block].astype(jnp.float32)
    gr_send[...] = total.reshape(places, capacity, unit).astype(jnp.bfloat16)
    to_experts(gr_send, gr_recv, 7)
    table_copy.wait()

    @pl.when(is_mid)
    def _():
        for part in range(PARTS):
            arrived(u_mid.at[part], 8 + part)
            target = upd_hbm.at[pl.ds(my_row, ROWS), column_at(my_col, part)]

            def forward(step, carry, part=part, target=target):
                peer = expert_peer(step)
                u_out[part, peer] = u_mid[part, partner_ref[0, peer]]
                pltpu.make_async_remote_copy(
                    src_ref=u_out.at[part, peer],
                    dst_ref=target,
                    send_sem=send_sem.at[8 + PARTS],
                    recv_sem=recv_sem.at[8 + PARTS],
                    device_id={"expert": peer},
                ).start()
                return carry

            lax.fori_loop(1, places, forward, 0)
            u_out[part, me] = u_mid[part, partner_ref[0, me]]
            pltpu.make_async_copy(u_out.at[part, me], target, recv_sem.at[8 + PARTS]).start()

    arrived(gr_recv, 7)
    back = gr_recv[...].astype(jnp.float32).reshape(slots, unit).astype(jnp.bfloat16)
    picked = dot(table[...], back, 0, 0)
    for choice in range(2):
        gate, up = gate_and_up(choice)
        sig = jax.nn.sigmoid(gate)
        grad_hidden = picked[choice * tok : (choice + 1) * tok]
        at = choice * 2 * unit
        ggu_ref[:, at : at + unit] = (
            grad_hidden * up * sig * (1.0 + gate * (1.0 - sig))
        ).astype(jnp.bfloat16)
        ggu_ref[:, at + unit : at + 2 * unit] = (grad_hidden * (gate * sig)).astype(jnp.bfloat16)
    for src, at in unsent:
        sent(src, at)

    arrived(upd_hbm, 8 + PARTS)

    @pl.when(is_mid)
    def _():
        for part in range(PARTS):
            sent(u_mid.at[part, pl.ds(0, row_groups * col_groups - 1)], 8 + part)
            sent(u_out.at[part, pl.ds(0, places - 1)], 8 + PARTS)

    @pl.when(jnp.logical_not(is_mid))
    def _():
        for part in range(PARTS):
            sent(u_mid.at[part, pl.ds(0, row_groups * col_groups)], 8 + part)


def local(
    swap_pairs,
    expert_ids,
    route_weights,
    gate_up,
    grad_out,
    down_weight,
    first_moment,
    second_moment,
):
    places = lax.axis_size("expert")
    n_hidden = lax.axis_size("hidden")
    tok, top = expert_ids.shape
    unit, depth = down_weight.shape[1:]
    feat = grad_out.shape[1]
    capacity = 2 * tok * top // places
    slots = places * capacity
    bf16 = jnp.bfloat16
    vmem = pl.BlockSpec(memory_space=pltpu.VMEM)
    anywhere = pl.BlockSpec(memory_space=pl.ANY)
    scratch = [
        ((unit, depth), bf16),
        ((unit, depth), bf16),
        ((unit, depth), bf16),
        ((slots, tok * top), bf16),
        ((places, capacity, unit), bf16),
        ((places, capacity, unit), bf16),
        ((places, capacity, feat), bf16),
        ((places, capacity, feat), bf16),
        ((n_hidden, unit, feat), bf16),
        ((n_hidden, unit, feat), bf16),
        ((slots, unit), bf16),
        ((n_hidden, slots, unit), bf16),
        ((places, capacity, feat), bf16),
        ((places, capacity, feat), bf16),
        ((n_hidden, unit, feat), bf16),
        ((n_hidden, unit, feat), bf16),
        ((n_hidden, slots, unit), bf16),
        ((n_hidden, slots, unit), bf16),
        ((places, capacity, unit), bf16),
        ((places, capacity, unit), bf16),
        ((unit, depth), bf16),
        ((PARTS, places, ROWS, COLS // PARTS), bf16),
        ((PARTS, places, ROWS, COLS // PARTS), bf16),
        ((1, 128), jnp.int32),
    ]
    combined, grads, update = pl.pallas_call(
        functools.partial(kernel, places, n_hidden, capacity),
        out_shape=(
            jax.ShapeDtypeStruct((feat, tok), bf16),
            jax.ShapeDtypeStruct((tok, top * 2 * unit), bf16),
            jax.ShapeDtypeStruct((unit, depth), bf16),
        ),
        in_specs=[vmem] * 5 + [anywhere] * 3,
        out_specs=(vmem, vmem, anywhere),
        scratch_shapes=[pltpu.VMEM(shape, kind) for shape, kind in scratch]
        + [
            pltpu.SMEM((1, 128), jnp.int32),
            pltpu.SemaphoreType.DMA((4,)),
            pltpu.SemaphoreType.DMA((9 + PARTS,)),
            pltpu.SemaphoreType.DMA((9 + PARTS,)),
        ],
        compiler_params=pltpu.CompilerParams(
            collective_id=0, has_side_effects=True, vmem_limit_bytes=VMEM_BYTES
        ),
    )(
        swap_pairs.T,
        expert_ids.T,
        route_weights.T,
        gate_up.reshape(tok, top * 2 * unit),
        grad_out.T,
        down_weight[0],
        first_moment[0],
        second_moment[0],
    )
    return combined.T, grads.reshape(tok, top, 2, unit), update[None]


def solution(mesh):
    placed = (
        P(),
        P("expert", None),
        P("expert", None),
        P("expert", None, None, "hidden"),
        P("expert", "hidden"),
        P("expert", "hidden", None),
        P("expert", "hidden", None),
        P("expert", "hidden", None),
    )
    return jax.shard_map(
        local,
        mesh=mesh,
        in_specs=placed,
        out_specs=(
            P("expert", "hidden"),
            P("expert", None, None, "hidden"),
            P("expert", "hidden", None),
        ),
        check_vma=False,
    )
```

```python
import functools

import jax
import jax.numpy as jnp
from jax import lax
from jax.experimental import pallas as pl
from jax.experimental.pallas import tpu as pltpu
from jax.sharding import PartitionSpec as P

first_decay = 0.9
second_decay = 0.95
adam_epsilon = 1e-08
ROWS = 16
COLS = 512
PARTS = 1
LANES = 128
VMEM_BYTES = 52 * 1024 * 1024


def dot(a, b, contract_a, contract_b):
    return lax.dot_general(
        a, b, (((contract_a,), (contract_b,)), ((), ())), preferred_element_type=jnp.float32
    )


def kernel(
    places,
    n_hidden,
    capacity,
    swap_ref,
    ids_ref,
    route_ref,
    acts_ref,
    gout_ref,
    w_hbm,
    m_hbm,
    v_hbm,
    comb_ref,
    ggu_ref,
    upd_hbm,
    w_all,
    m_here,
    v_here,
    table,
    h_send,
    h_recv,
    g_send,
    g_recv,
    w_recv,
    h_own,
    h_all,
    y_send,
    y_recv,
    gw_send,
    gw_recv,
    gh_send,
    gh_recv,
    gr_send,
    gr_recv,
    u_here,
    u_mid,
    u_out,
    partner_row,
    partner_ref,
    local_sem,
    send_sem,
    recv_sem,
):
    me = lax.axis_index("expert")
    mine = lax.axis_index("hidden")
    tok = ids_ref.shape[1]
    count = 2 * tok
    slots = places * capacity
    unit = h_own.shape[1]
    feat = gout_ref.shape[0]
    row_groups = m_here.shape[0] // ROWS
    col_groups = m_here.shape[1] // COLS
    stride = places // row_groups

    def far_first(at, step, length):
        near = length - step
        half = (near + 1) // 2
        return lax.rem(at + half + (1 - lax.rem(near, 2)) * (length - 2 * half), length)

    def expert_peer(step):
        return far_first(me, step, places)

    def hidden_peer(step):
        return lax.rem(mine + step, n_hidden)

    barrier = pltpu.get_barrier_semaphore()

    def greet_expert(step, carry):
        pl.semaphore_signal(barrier, inc=1, device_id={"expert": expert_peer(step)})
        return carry

    def greet_hidden(step, carry):
        pl.semaphore_signal(barrier, inc=1, device_id={"hidden": hidden_peer(step)})
        return carry

    lax.fori_loop(1, places, greet_expert, 0)
    lax.fori_loop(1, n_hidden, greet_hidden, 0)

    loads = [
        pltpu.make_async_copy(src, dst, local_sem.at[at])
        for at, (src, dst) in enumerate(((m_hbm, m_here), (v_hbm, v_here)))
    ]
    for load in loads:
        load.start()

    ids = jnp.concatenate([ids_ref[0:1, :], ids_ref[1:2, :]], axis=1)
    hot = (lax.broadcasted_iota(jnp.int32, (places, count), 0) == ids).astype(jnp.float32)
    earlier = (
        lax.broadcasted_iota(jnp.int32, (count, count), 0)
        < lax.broadcasted_iota(jnp.int32, (count, count), 1)
    ).astype(jnp.bfloat16)
    before = dot(hot.astype(jnp.bfloat16), earlier, 1, 0)
    rank = jnp.sum(before * hot, axis=0, keepdims=True).astype(jnp.int32)
    slot = ids * capacity + rank
    table[...] = (lax.broadcasted_iota(jnp.int32, (slots, count), 0) == slot).astype(jnp.bfloat16)

    def gate_and_up(choice):
        at = choice * 2 * unit
        gate = acts_ref[:, at : at + unit].astype(jnp.float32)
        up = acts_ref[:, at + unit : at + 2 * unit].astype(jnp.float32)
        return gate, up

    rows = []
    for choice in range(2):
        gate, up = gate_and_up(choice)
        rows.append((gate * jax.nn.sigmoid(gate) * up).astype(jnp.bfloat16))
    placed = dot(table[...], jnp.concatenate(rows, axis=0), 1, 0)
    h_send[...] = placed.reshape(places, capacity, unit).astype(jnp.bfloat16)

    unsent = []

    def arrived(dst, at):
        pltpu.make_async_copy(dst, dst, recv_sem.at[at]).wait()

    def sent(src, at):
        pltpu.make_async_copy(src, src, send_sem.at[at]).wait()

    def to_experts(src, dst, at, first=1, last=places):
        def send(step, carry):
            peer = expert_peer(step)
            pltpu.make_async_remote_copy(
                src_ref=src.at[peer],
                dst_ref=dst.at[me],
                send_sem=send_sem.at[at],
                recv_sem=recv_sem.at[at],
                device_id={"expert": peer},
            ).start()
            return carry

        lax.fori_loop(first, last, send, 0)
        if last == places:
            pltpu.make_async_copy(src.at[me], dst.at[me], recv_sem.at[at]).start()
            unsent.append((dst.at[pl.ds(0, places - 1)], at))

    def to_hidden(pick, dst, at):
        def send(step, carry):
            peer = hidden_peer(step)
            pltpu.make_async_remote_copy(
                src_ref=pick(peer),
                dst_ref=dst.at[mine],
                send_sem=send_sem.at[at],
                recv_sem=recv_sem.at[at],
                device_id={"hidden": peer},
            ).start()
            return carry

        lax.fori_loop(1, n_hidden, send, 0)
        pltpu.make_async_copy(pick(mine), dst.at[mine], recv_sem.at[at]).start()
        unsent.append((dst.at[pl.ds(0, n_hidden - 1)], at))

    rows = [
        (route_ref[choice : choice + 1, :] * gout_ref[...].astype(jnp.float32)).astype(jnp.bfloat16)
        for choice in range(2)
    ]
    placed = dot(table[...], jnp.concatenate(rows, axis=1), 1, 1)
    g_send[...] = placed.reshape(places, capacity, feat).astype(jnp.bfloat16)
    def send_blocks(product, src, dst, at):
        def send(step, carry):
            peer = hidden_peer(step)
            src[peer] = product(peer).astype(jnp.bfloat16)
            pltpu.make_async_remote_copy(
                src_ref=src.at[peer],
                dst_ref=dst.at[mine],
                send_sem=send_sem.at[at],
                recv_sem=recv_sem.at[at],
                device_id={"hidden": peer},
            ).start()
            return carry

        lax.fori_loop(1, n_hidden, send, 0)
        src[mine] = product(mine).astype(jnp.bfloat16)
        pltpu.make_async_copy(src.at[mine], dst.at[mine], recv_sem.at[at]).start()
        unsent.append((dst.at[pl.ds(0, n_hidden - 1)], at))

    pl.semaphore_wait(barrier, places + n_hidden - 2)
    span = w_recv.shape[2]

    def weight_window(peer):
        at = pl.multiple_of(peer * feat // LANES * LANES, LANES)
        return w_hbm.at[:, pl.ds(at, span)]

    to_hidden(weight_window, w_recv, 1)
    to_experts(h_send, h_recv, 0)
    to_experts(g_send, g_recv, 2)

    place = lax.broadcasted_iota(jnp.int32, (128, swap_ref.shape[1]), 0)
    left, right = swap_ref[0:1, :], swap_ref[1:2, :]
    trades = jnp.where(place == left, right, 0) + jnp.where(place == right, left, 0)
    trades = jnp.sum(trades, axis=1, keepdims=True)
    partner_row[...] = jnp.broadcast_to(trades, (128, 128)).T[0:1, :]
    table_copy = pltpu.make_async_copy(partner_row, partner_ref, local_sem.at[3])
    table_copy.start()

    arrived(h_recv, 0)
    h_own[...] = h_recv[...].astype(jnp.float32).reshape(slots, unit).astype(jnp.bfloat16)
    to_hidden(lambda peer: h_own, h_all, 3)
    arrived(w_recv, 1)
    shift = span - feat

    @pl.when(lax.rem(mine * feat, LANES) == 0)
    def _():
        w_all[...] = w_recv[:, :, :feat]

    @pl.when(lax.rem(mine * feat, LANES) != 0)
    def _():
        w_all[...] = w_recv[:, :, shift:]

    arrived(h_all, 3)
    h_cat = jnp.concatenate([h_all[block] for block in range(n_hidden)], axis=1)
    y_send[...] = dot(h_cat, w_all[...].reshape(n_hidden * unit, feat), 1, 0).reshape(places, capacity, feat).astype(jnp.bfloat16)
    to_experts(y_send, y_recv, 4, 1, places // 2)
    arrived(g_recv, 2)
    grads = g_recv[...].astype(jnp.float32).reshape(slots, feat).astype(jnp.bfloat16)
    send_blocks(lambda block: dot(h_all[block], grads, 0, 0), gw_send, gw_recv, 5)
    to_experts(y_send, y_recv, 4, places // 2, places)

    arrived(gw_recv, 5)
    for load in loads:
        load.wait()
    is_mid = lax.rem(me, stride) < col_groups
    my_row = pl.multiple_of((me // stride) * ROWS, ROWS)
    my_col = lax.rem(me, stride) * COLS
    wide = COLS // PARTS

    def column_at(base, part):
        return pl.ds(pl.multiple_of(base + part * wide, wide), wide)

    def send_rows(group, part):
        at = pl.multiple_of(group * ROWS, ROWS)

        def send(col, carry):
            peer = group * stride + col
            chunk = u_here.at[pl.ds(at, ROWS), column_at(col * COLS, part)]

            @pl.when(peer == me)
            def _():
                pltpu.make_async_copy(chunk, u_mid.at[part, me], recv_sem.at[8 + part]).start()

            @pl.when(peer != me)
            def _():
                pltpu.make_async_remote_copy(
                    src_ref=chunk,
                    dst_ref=u_mid.at[part, me],
                    send_sem=send_sem.at[8 + part],
                    recv_sem=recv_sem.at[8 + part],
                    device_id={"expert": peer},
                ).start()

            return carry

        lax.fori_loop(0, col_groups, send, 0)

    def row_group(step):
        return far_first(me // stride, step, row_groups)

    def update_rows(step, carry):
        group = row_group(step)
        at = pl.multiple_of(group * ROWS, ROWS)
        for pair in range(n_hidden // 2):
            span = slice(pair * 2 * feat, (pair + 1) * 2 * feat)
            grad = jnp.concatenate(
                [
                    gw_recv[2 * pair, pl.ds(at, ROWS), :],
                    gw_recv[2 * pair + 1, pl.ds(at, ROWS), :],
                ],
                axis=1,
            ).astype(jnp.float32)
            first = m_here[pl.ds(at, ROWS), span].astype(jnp.float32)
            second = v_here[pl.ds(at, ROWS), span].astype(jnp.float32)
            first_new = first_decay * first + (1.0 - first_decay) * grad
            second_new = second_decay * second + (1.0 - second_decay) * grad * grad
            u_here[pl.ds(at, ROWS), span] = (
                first_new / (jnp.sqrt(second_new) + adam_epsilon)
            ).astype(jnp.bfloat16)
        send_rows(group, 0)
        return carry

    lax.fori_loop(1, row_groups + 1, update_rows, 0)
    send_blocks(lambda block: dot(grads, w_all[block], 1, 1), gh_send, gh_recv, 6)

    arrived(y_recv, 4)
    back = y_recv[...].astype(jnp.float32).reshape(slots, feat).astype(jnp.bfloat16)
    picked = dot(back, table[...], 0, 0)
    comb_ref[...] = (
        route_ref[0:1, :] * picked[:, :tok] + route_ref[1:2, :] * picked[:, tok:]
    ).astype(jnp.bfloat16)
    arrived(gh_recv, 6)
    total = gh_recv[0].astype(jnp.float32)
    for block in range(1, n_hidden):
        total = total + gh_recv[block].astype(jnp.float32)
    gr_send[...] = total.reshape(places, capacity, unit).astype(jnp.bfloat16)

    @pl.when(is_mid)
    def _():
        for part in range(PARTS):
            sent(u_mid.at[part, pl.ds(0, row_groups * col_groups - 1)], 8 + part)

    @pl.when(jnp.logical_not(is_mid))
    def _():
        for part in range(PARTS):
            sent(u_mid.at[part, pl.ds(0, row_groups * col_groups)], 8 + part)

    to_experts(gr_send, gr_recv, 7)
    table_copy.wait()

    @pl.when(is_mid)
    def _():
        for part in range(PARTS):
            arrived(u_mid.at[part], 8 + part)
            target = upd_hbm.at[pl.ds(my_row, ROWS), column_at(my_col, part)]

            def forward(step, carry, part=part, target=target):
                peer = expert_peer(step)
                u_out[part, peer] = u_mid[part, partner_ref[0, peer]]
                pltpu.make_async_remote_copy(
                    src_ref=u_out.at[part, peer],
                    dst_ref=target,
                    send_sem=send_sem.at[8 + PARTS],
                    recv_sem=recv_sem.at[8 + PARTS],
                    device_id={"expert": peer},
                ).start()
                return carry

            lax.fori_loop(1, places, forward, 0)
            u_out[part, me] = u_mid[part, partner_ref[0, me]]
            pltpu.make_async_copy(u_out.at[part, me], target, recv_sem.at[8 + PARTS]).start()

    arrived(gr_recv, 7)
    back = gr_recv[...].astype(jnp.float32).reshape(slots, unit).astype(jnp.bfloat16)
    picked = dot(table[...], back, 0, 0)
    for choice in range(2):
        gate, up = gate_and_up(choice)
        sig = jax.nn.sigmoid(gate)
        grad_hidden = picked[choice * tok : (choice + 1) * tok]
        at = choice * 2 * unit
        ggu_ref[:, at : at + unit] = (
            grad_hidden * up * sig * (1.0 + gate * (1.0 - sig))
        ).astype(jnp.bfloat16)
        ggu_ref[:, at + unit : at + 2 * unit] = (grad_hidden * (gate * sig)).astype(jnp.bfloat16)
    for src, at in unsent:
        sent(src, at)

    arrived(upd_hbm, 8 + PARTS)

    @pl.when(is_mid)
    def _():
        for part in range(PARTS):
            sent(u_out.at[part, pl.ds(0, places - 1)], 8 + PARTS)


def local(
    swap_pairs,
    expert_ids,
    route_weights,
    gate_up,
    grad_out,
    down_weight,
    first_moment,
    second_moment,
):
    places = lax.axis_size("expert")
    n_hidden = lax.axis_size("hidden")
    tok, top = expert_ids.shape
    unit, depth = down_weight.shape[1:]
    feat = grad_out.shape[1]
    capacity = 2 * tok * top // places
    slots = places * capacity
    bf16 = jnp.bfloat16
    vmem = pl.BlockSpec(memory_space=pltpu.VMEM)
    anywhere = pl.BlockSpec(memory_space=pl.ANY)
    scratch = [
        ((n_hidden, unit, feat), bf16),
        ((unit, depth), bf16),
        ((unit, depth), bf16),
        ((slots, tok * top), bf16),
        ((places, capacity, unit), bf16),
        ((places, capacity, unit), bf16),
        ((places, capacity, feat), bf16),
        ((places, capacity, feat), bf16),
        ((n_hidden, unit, -(-feat // LANES) * LANES), bf16),
        ((slots, unit), bf16),
        ((n_hidden, slots, unit), bf16),
        ((places, capacity, feat), bf16),
        ((places, capacity, feat), bf16),
        ((n_hidden, unit, feat), bf16),
        ((n_hidden, unit, feat), bf16),
        ((n_hidden, slots, unit), bf16),
        ((n_hidden, slots, unit), bf16),
        ((places, capacity, unit), bf16),
        ((places, capacity, unit), bf16),
        ((unit, depth), bf16),
        ((PARTS, places, ROWS, COLS // PARTS), bf16),
        ((PARTS, places, ROWS, COLS // PARTS), bf16),
        ((1, 128), jnp.int32),
    ]
    combined, grads, update = pl.pallas_call(
        functools.partial(kernel, places, n_hidden, capacity),
        out_shape=(
            jax.ShapeDtypeStruct((feat, tok), bf16),
            jax.ShapeDtypeStruct((tok, top * 2 * unit), bf16),
            jax.ShapeDtypeStruct((unit, depth), bf16),
        ),
        in_specs=[vmem] * 5 + [anywhere] * 3,
        out_specs=(vmem, vmem, anywhere),
        scratch_shapes=[pltpu.VMEM(shape, kind) for shape, kind in scratch]
        + [
            pltpu.SMEM((1, 128), jnp.int32),
            pltpu.SemaphoreType.DMA((4,)),
            pltpu.SemaphoreType.DMA((9 + PARTS,)),
            pltpu.SemaphoreType.DMA((9 + PARTS,)),
        ],
        compiler_params=pltpu.CompilerParams(
            collective_id=0, has_side_effects=True, vmem_limit_bytes=VMEM_BYTES
        ),
    )(
        swap_pairs.T,
        expert_ids.T,
        route_weights.T,
        gate_up.reshape(tok, top * 2 * unit),
        grad_out.T,
        down_weight[0],
        first_moment[0],
        second_moment[0],
    )
    return combined.T, grads.reshape(tok, top, 2, unit), update[None]


def solution(mesh):
    placed = (
        P(),
        P("expert", None),
        P("expert", None),
        P("expert", None, None, "hidden"),
        P("expert", "hidden"),
        P("expert", "hidden", None),
        P("expert", "hidden", None),
        P("expert", "hidden", None),
    )
    return jax.shard_map(
        local,
        mesh=mesh,
        in_specs=placed,
        out_specs=(
            P("expert", "hidden"),
            P("expert", None, None, "hidden"),
            P("expert", "hidden", None),
        ),
        check_vma=False,
    )
```

```python
import functools

import jax
import jax.numpy as jnp
from jax import lax
from jax.experimental import pallas as pl
from jax.experimental.pallas import tpu as pltpu
from jax.sharding import PartitionSpec as P

first_decay = 0.9
second_decay = 0.95
adam_epsilon = 1e-08
ROWS = 16
COLS = 512
PARTS = 1
LANES = 128
VMEM_BYTES = 52 * 1024 * 1024


def dot(a, b, contract_a, contract_b):
    return lax.dot_general(
        a, b, (((contract_a,), (contract_b,)), ((), ())), preferred_element_type=jnp.float32
    )


def kernel(
    places,
    n_hidden,
    capacity,
    swap_ref,
    ids_ref,
    route_ref,
    acts_ref,
    gout_ref,
    w_hbm,
    m_hbm,
    v_hbm,
    comb_ref,
    ggu_ref,
    upd_hbm,
    w_all,
    m_here,
    v_here,
    table,
    h_send,
    h_recv,
    g_send,
    g_recv,
    w_recv,
    h_own,
    h_all,
    y_send,
    y_recv,
    gw_send,
    gw_recv,
    gh_send,
    gh_recv,
    gr_send,
    gr_recv,
    u_here,
    u_mid,
    u_out,
    partner_row,
    partner_ref,
    local_sem,
    send_sem,
    recv_sem,
):
    me = lax.axis_index("expert")
    mine = lax.axis_index("hidden")
    tok = ids_ref.shape[1]
    count = 2 * tok
    slots = places * capacity
    unit = h_own.shape[1]
    feat = gout_ref.shape[0]
    row_groups = m_here.shape[0] // ROWS
    col_groups = m_here.shape[1] // COLS
    stride = places // row_groups

    def far_first(at, step, length):
        near = length - step
        half = (near + 1) // 2
        return lax.rem(at + half + (1 - lax.rem(near, 2)) * (length - 2 * half), length)

    def expert_peer(step):
        return far_first(me, step, places)

    def hidden_peer(step):
        return lax.rem(mine + step, n_hidden)

    barrier = pltpu.get_barrier_semaphore()

    def greet_expert(step, carry):
        pl.semaphore_signal(barrier, inc=1, device_id={"expert": expert_peer(step)})
        return carry

    def greet_hidden(step, carry):
        pl.semaphore_signal(barrier, inc=1, device_id={"hidden": hidden_peer(step)})
        return carry

    lax.fori_loop(1, places, greet_expert, 0)
    lax.fori_loop(1, n_hidden, greet_hidden, 0)

    loads = [
        pltpu.make_async_copy(src, dst, local_sem.at[at])
        for at, (src, dst) in enumerate(((m_hbm, m_here), (v_hbm, v_here)))
    ]
    for load in loads:
        load.start()

    ids = jnp.concatenate([ids_ref[0:1, :], ids_ref[1:2, :]], axis=1)
    hot = (lax.broadcasted_iota(jnp.int32, (places, count), 0) == ids).astype(jnp.float32)
    earlier = (
        lax.broadcasted_iota(jnp.int32, (count, count), 0)
        < lax.broadcasted_iota(jnp.int32, (count, count), 1)
    ).astype(jnp.bfloat16)
    before = dot(hot.astype(jnp.bfloat16), earlier, 1, 0)
    rank = jnp.sum(before * hot, axis=0, keepdims=True).astype(jnp.int32)
    slot = ids * capacity + rank
    table[...] = (lax.broadcasted_iota(jnp.int32, (slots, count), 0) == slot).astype(jnp.bfloat16)

    def gate_and_up(choice):
        at = choice * 2 * unit
        gate = acts_ref[:, at : at + unit].astype(jnp.float32)
        up = acts_ref[:, at + unit : at + 2 * unit].astype(jnp.float32)
        return gate, up

    rows = []
    for choice in range(2):
        gate, up = gate_and_up(choice)
        rows.append((gate * jax.nn.sigmoid(gate) * up).astype(jnp.bfloat16))
    placed = dot(table[...], jnp.concatenate(rows, axis=0), 1, 0)
    h_send[...] = placed.reshape(places, capacity, unit).astype(jnp.bfloat16)

    unsent = []

    def arrived(dst, at):
        pltpu.make_async_copy(dst, dst, recv_sem.at[at]).wait()

    def sent(src, at):
        pltpu.make_async_copy(src, src, send_sem.at[at]).wait()

    def to_experts(src, dst, at, first=1, last=places):
        def send(step, carry):
            peer = expert_peer(step)
            pltpu.make_async_remote_copy(
                src_ref=src.at[peer],
                dst_ref=dst.at[me],
                send_sem=send_sem.at[at],
                recv_sem=recv_sem.at[at],
                device_id={"expert": peer},
            ).start()
            return carry

        lax.fori_loop(first, last, send, 0)
        if last == places:
            pltpu.make_async_copy(src.at[me], dst.at[me], recv_sem.at[at]).start()
            unsent.append((dst.at[pl.ds(0, places - 1)], at))

    def to_hidden(pick, dst, at):
        def send(step, carry):
            peer = hidden_peer(step)
            pltpu.make_async_remote_copy(
                src_ref=pick(peer),
                dst_ref=dst.at[mine],
                send_sem=send_sem.at[at],
                recv_sem=recv_sem.at[at],
                device_id={"hidden": peer},
            ).start()
            return carry

        lax.fori_loop(1, n_hidden, send, 0)
        pltpu.make_async_copy(pick(mine), dst.at[mine], recv_sem.at[at]).start()
        unsent.append((dst.at[pl.ds(0, n_hidden - 1)], at))

    rows = [
        (route_ref[choice : choice + 1, :] * gout_ref[...].astype(jnp.float32)).astype(jnp.bfloat16)
        for choice in range(2)
    ]
    placed = dot(table[...], jnp.concatenate(rows, axis=1), 1, 1)
    g_send[...] = placed.reshape(places, capacity, feat).astype(jnp.bfloat16)
    def send_blocks(product, src, dst, at):
        def send(step, carry):
            peer = hidden_peer(step)
            src[peer] = product(peer).astype(jnp.bfloat16)
            pltpu.make_async_remote_copy(
                src_ref=src.at[peer],
                dst_ref=dst.at[mine],
                send_sem=send_sem.at[at],
                recv_sem=recv_sem.at[at],
                device_id={"hidden": peer},
            ).start()
            return carry

        lax.fori_loop(1, n_hidden, send, 0)
        src[mine] = product(mine).astype(jnp.bfloat16)
        pltpu.make_async_copy(src.at[mine], dst.at[mine], recv_sem.at[at]).start()
        unsent.append((dst.at[pl.ds(0, n_hidden - 1)], at))

    pl.semaphore_wait(barrier, places + n_hidden - 2)
    span = w_recv.shape[2]

    def weight_window(peer):
        at = pl.multiple_of(peer * feat // LANES * LANES, LANES)
        return w_hbm.at[:, pl.ds(at, span)]

    to_hidden(weight_window, w_recv, 1)
    to_experts(h_send, h_recv, 0)
    to_experts(g_send, g_recv, 2)

    place = lax.broadcasted_iota(jnp.int32, (128, swap_ref.shape[1]), 0)
    left, right = swap_ref[0:1, :], swap_ref[1:2, :]
    trades = jnp.where(place == left, right, 0) + jnp.where(place == right, left, 0)
    trades = jnp.sum(trades, axis=1, keepdims=True)
    partner_row[...] = jnp.broadcast_to(trades, (128, 128)).T[0:1, :]
    table_copy = pltpu.make_async_copy(partner_row, partner_ref, local_sem.at[3])
    table_copy.start()

    arrived(h_recv, 0)
    h_own[...] = h_recv[...].astype(jnp.float32).reshape(slots, unit).astype(jnp.bfloat16)
    to_hidden(lambda peer: h_own, h_all, 3)
    arrived(w_recv, 1)
    shift = span - feat

    @pl.when(lax.rem(mine * feat, LANES) == 0)
    def _():
        w_all[...] = w_recv[:, :, :feat]

    @pl.when(lax.rem(mine * feat, LANES) != 0)
    def _():
        w_all[...] = w_recv[:, :, shift:]

    arrived(h_all, 3)
    h_cat = jnp.concatenate([h_all[block] for block in range(n_hidden)], axis=1)
    y_send[...] = dot(h_cat, w_all[...].reshape(n_hidden * unit, feat), 1, 0).reshape(places, capacity, feat).astype(jnp.bfloat16)
    to_experts(y_send, y_recv, 4, 1, places // 2)
    arrived(g_recv, 2)
    grads = g_recv[...].astype(jnp.float32).reshape(slots, feat).astype(jnp.bfloat16)
    send_blocks(lambda block: dot(h_all[block], grads, 0, 0), gw_send, gw_recv, 5)
    to_experts(y_send, y_recv, 4, places // 2, places)

    arrived(gw_recv, 5)
    for load in loads:
        load.wait()

    def spare_seat(group):
        return stride - 1 - 2 * lax.rem(group, stride // 2)

    def past_spare(at, group):
        return (at + stride - spare_seat(group)) // stride

    my_group, my_seat = me // stride, lax.rem(me, stride)
    is_mid = my_seat != spare_seat(my_group)
    my_row = pl.multiple_of(my_group * ROWS, ROWS)
    my_col = (my_seat - past_spare(my_seat, my_group)) * COLS
    wide = COLS // PARTS

    def column_at(base, part):
        return pl.ds(pl.multiple_of(base + part * wide, wide), wide)

    def send_rows(group, part):
        at = pl.multiple_of(group * ROWS, ROWS)

        def send(col, carry):
            peer = group * stride + col + past_spare(col, group)
            chunk = u_here.at[pl.ds(at, ROWS), column_at(col * COLS, part)]

            @pl.when(peer == me)
            def _():
                pltpu.make_async_copy(chunk, u_mid.at[part, me], recv_sem.at[8 + part]).start()

            @pl.when(peer != me)
            def _():
                pltpu.make_async_remote_copy(
                    src_ref=chunk,
                    dst_ref=u_mid.at[part, me],
                    send_sem=send_sem.at[8 + part],
                    recv_sem=recv_sem.at[8 + part],
                    device_id={"expert": peer},
                ).start()

            return carry

        lax.fori_loop(0, col_groups, send, 0)

    def row_group(step):
        return far_first(me // stride, step, row_groups)

    def update_rows(step, carry):
        group = row_group(step)
        at = pl.multiple_of(group * ROWS, ROWS)
        for pair in range(n_hidden // 2):
            span = slice(pair * 2 * feat, (pair + 1) * 2 * feat)
            grad = jnp.concatenate(
                [
                    gw_recv[2 * pair, pl.ds(at, ROWS), :],
                    gw_recv[2 * pair + 1, pl.ds(at, ROWS), :],
                ],
                axis=1,
            ).astype(jnp.float32)
            first = m_here[pl.ds(at, ROWS), span].astype(jnp.float32)
            second = v_here[pl.ds(at, ROWS), span].astype(jnp.float32)
            first_new = first_decay * first + (1.0 - first_decay) * grad
            second_new = second_decay * second + (1.0 - second_decay) * grad * grad
            u_here[pl.ds(at, ROWS), span] = (
                first_new / (jnp.sqrt(second_new) + adam_epsilon)
            ).astype(jnp.bfloat16)
        send_rows(group, 0)
        return carry

    lax.fori_loop(1, row_groups + 1, update_rows, 0)
    send_blocks(lambda block: dot(grads, w_all[block], 1, 1), gh_send, gh_recv, 6)

    arrived(y_recv, 4)
    back = y_recv[...].astype(jnp.float32).reshape(slots, feat).astype(jnp.bfloat16)
    picked = dot(back, table[...], 0, 0)
    comb_ref[...] = (
        route_ref[0:1, :] * picked[:, :tok] + route_ref[1:2, :] * picked[:, tok:]
    ).astype(jnp.bfloat16)
    arrived(gh_recv, 6)
    total = gh_recv[0].astype(jnp.float32)
    for block in range(1, n_hidden):
        total = total + gh_recv[block].astype(jnp.float32)
    gr_send[...] = total.reshape(places, capacity, unit).astype(jnp.bfloat16)

    @pl.when(is_mid)
    def _():
        for part in range(PARTS):
            sent(u_mid.at[part, pl.ds(0, row_groups * col_groups - 1)], 8 + part)

    @pl.when(jnp.logical_not(is_mid))
    def _():
        for part in range(PARTS):
            sent(u_mid.at[part, pl.ds(0, row_groups * col_groups)], 8 + part)

    to_experts(gr_send, gr_recv, 7)
    table_copy.wait()

    @pl.when(is_mid)
    def _():
        for part in range(PARTS):
            arrived(u_mid.at[part], 8 + part)
            target = upd_hbm.at[pl.ds(my_row, ROWS), column_at(my_col, part)]

            def forward(step, carry, part=part, target=target):
                peer = expert_peer(step)
                u_out[part, peer] = u_mid[part, partner_ref[0, peer]]
                pltpu.make_async_remote_copy(
                    src_ref=u_out.at[part, peer],
                    dst_ref=target,
                    send_sem=send_sem.at[8 + PARTS],
                    recv_sem=recv_sem.at[8 + PARTS],
                    device_id={"expert": peer},
                ).start()
                return carry

            lax.fori_loop(1, places, forward, 0)
            u_out[part, me] = u_mid[part, partner_ref[0, me]]
            pltpu.make_async_copy(u_out.at[part, me], target, recv_sem.at[8 + PARTS]).start()

    arrived(gr_recv, 7)
    back = gr_recv[...].astype(jnp.float32).reshape(slots, unit).astype(jnp.bfloat16)
    picked = dot(table[...], back, 0, 0)
    for choice in range(2):
        gate, up = gate_and_up(choice)
        sig = jax.nn.sigmoid(gate)
        grad_hidden = picked[choice * tok : (choice + 1) * tok]
        at = choice * 2 * unit
        ggu_ref[:, at : at + unit] = (
            grad_hidden * up * sig * (1.0 + gate * (1.0 - sig))
        ).astype(jnp.bfloat16)
        ggu_ref[:, at + unit : at + 2 * unit] = (grad_hidden * (gate * sig)).astype(jnp.bfloat16)
    for src, at in unsent:
        sent(src, at)

    arrived(upd_hbm, 8 + PARTS)

    @pl.when(is_mid)
    def _():
        for part in range(PARTS):
            sent(u_out.at[part, pl.ds(0, places - 1)], 8 + PARTS)


def local(
    swap_pairs,
    expert_ids,
    route_weights,
    gate_up,
    grad_out,
    down_weight,
    first_moment,
    second_moment,
):
    places = lax.axis_size("expert")
    n_hidden = lax.axis_size("hidden")
    tok, top = expert_ids.shape
    unit, depth = down_weight.shape[1:]
    feat = grad_out.shape[1]
    capacity = 2 * tok * top // places
    slots = places * capacity
    bf16 = jnp.bfloat16
    vmem = pl.BlockSpec(memory_space=pltpu.VMEM)
    anywhere = pl.BlockSpec(memory_space=pl.ANY)
    scratch = [
        ((n_hidden, unit, feat), bf16),
        ((unit, depth), bf16),
        ((unit, depth), bf16),
        ((slots, tok * top), bf16),
        ((places, capacity, unit), bf16),
        ((places, capacity, unit), bf16),
        ((places, capacity, feat), bf16),
        ((places, capacity, feat), bf16),
        ((n_hidden, unit, -(-feat // LANES) * LANES), bf16),
        ((slots, unit), bf16),
        ((n_hidden, slots, unit), bf16),
        ((places, capacity, feat), bf16),
        ((places, capacity, feat), bf16),
        ((n_hidden, unit, feat), bf16),
        ((n_hidden, unit, feat), bf16),
        ((n_hidden, slots, unit), bf16),
        ((n_hidden, slots, unit), bf16),
        ((places, capacity, unit), bf16),
        ((places, capacity, unit), bf16),
        ((unit, depth), bf16),
        ((PARTS, places, ROWS, COLS // PARTS), bf16),
        ((PARTS, places, ROWS, COLS // PARTS), bf16),
        ((1, 128), jnp.int32),
    ]
    combined, grads, update = pl.pallas_call(
        functools.partial(kernel, places, n_hidden, capacity),
        out_shape=(
            jax.ShapeDtypeStruct((feat, tok), bf16),
            jax.ShapeDtypeStruct((tok, top * 2 * unit), bf16),
            jax.ShapeDtypeStruct((unit, depth), bf16),
        ),
        in_specs=[vmem] * 5 + [anywhere] * 3,
        out_specs=(vmem, vmem, anywhere),
        scratch_shapes=[pltpu.VMEM(shape, kind) for shape, kind in scratch]
        + [
            pltpu.SMEM((1, 128), jnp.int32),
            pltpu.SemaphoreType.DMA((4,)),
            pltpu.SemaphoreType.DMA((9 + PARTS,)),
            pltpu.SemaphoreType.DMA((9 + PARTS,)),
        ],
        compiler_params=pltpu.CompilerParams(
            collective_id=0, has_side_effects=True, vmem_limit_bytes=VMEM_BYTES
        ),
    )(
        swap_pairs.T,
        expert_ids.T,
        route_weights.T,
        gate_up.reshape(tok, top * 2 * unit),
        grad_out.T,
        down_weight[0],
        first_moment[0],
        second_moment[0],
    )
    return combined.T, grads.reshape(tok, top, 2, unit), update[None]


def solution(mesh):
    placed = (
        P(),
        P("expert", None),
        P("expert", None),
        P("expert", None, None, "hidden"),
        P("expert", "hidden"),
        P("expert", "hidden", None),
        P("expert", "hidden", None),
        P("expert", "hidden", None),
    )
    return jax.shard_map(
        local,
        mesh=mesh,
        in_specs=placed,
        out_specs=(
            P("expert", "hidden"),
            P("expert", None, None, "hidden"),
            P("expert", "hidden", None),
        ),
        check_vma=False,
    )
```

```python
import functools

import jax
import jax.numpy as jnp
from jax import lax
from jax.experimental import pallas as pl
from jax.experimental.pallas import tpu as pltpu
from jax.sharding import PartitionSpec as P

first_decay = 0.9
second_decay = 0.95
adam_epsilon = 1e-08
ROWS = 16
COLS = 512
PARTS = 1
LANES = 128
GRADS = 12
OUTPUTS = 16
VMEM_BYTES = 52 * 1024 * 1024


def dot(a, b, contract_a, contract_b):
    return lax.dot_general(
        a, b, (((contract_a,), (contract_b,)), ((), ())), preferred_element_type=jnp.float32
    )


def kernel(
    places,
    n_hidden,
    capacity,
    swap_ref,
    ids_ref,
    route_ref,
    acts_ref,
    gout_ref,
    w_hbm,
    m_hbm,
    v_hbm,
    comb_ref,
    ggu_ref,
    upd_hbm,
    w_all,
    m_here,
    v_here,
    table,
    h_send,
    h_recv,
    g_send,
    g_recv,
    g_rows,
    w_recv,
    h_own,
    h_all,
    y_send,
    y_recv,
    y_rows,
    gw_send,
    gw_recv,
    gh_send,
    gh_recv,
    gr_send,
    gr_recv,
    u_here,
    u_mid,
    u_out,
    partner_row,
    partner_ref,
    local_sem,
    send_sem,
    recv_sem,
):
    me = lax.axis_index("expert")
    mine = lax.axis_index("hidden")
    tok = ids_ref.shape[1]
    count = 2 * tok
    slots = places * capacity
    unit = h_own.shape[1]
    feat = gout_ref.shape[0]
    row_groups = m_here.shape[0] // ROWS
    col_groups = m_here.shape[1] // COLS
    stride = places // row_groups

    def far_first(at, step, length):
        near = length - step
        half = (near + 1) // 2
        return lax.rem(at + half + (1 - lax.rem(near, 2)) * (length - 2 * half), length)

    def expert_peer(step):
        return far_first(me, step, places)

    def hidden_peer(step):
        return lax.rem(mine + step, n_hidden)

    barrier = pltpu.get_barrier_semaphore()

    def greet_expert(step, carry):
        pl.semaphore_signal(barrier, inc=1, device_id={"expert": expert_peer(step)})
        return carry

    def greet_hidden(step, carry):
        pl.semaphore_signal(barrier, inc=1, device_id={"hidden": hidden_peer(step)})
        return carry

    lax.fori_loop(1, places, greet_expert, 0)
    lax.fori_loop(1, n_hidden, greet_hidden, 0)

    loads = [
        pltpu.make_async_copy(src, dst, local_sem.at[at])
        for at, (src, dst) in enumerate(((m_hbm, m_here), (v_hbm, v_here)))
    ]
    for load in loads:
        load.start()

    ids = jnp.concatenate([ids_ref[0:1, :], ids_ref[1:2, :]], axis=1)
    hot = (lax.broadcasted_iota(jnp.int32, (places, count), 0) == ids).astype(jnp.float32)
    earlier = (
        lax.broadcasted_iota(jnp.int32, (count, count), 0)
        < lax.broadcasted_iota(jnp.int32, (count, count), 1)
    ).astype(jnp.bfloat16)
    before = dot(hot.astype(jnp.bfloat16), earlier, 1, 0)
    rank = jnp.sum(before * hot, axis=0, keepdims=True).astype(jnp.int32)
    slot = ids * capacity + rank
    table[...] = (lax.broadcasted_iota(jnp.int32, (slots, count), 0) == slot).astype(jnp.bfloat16)

    def gate_and_up(choice):
        at = choice * 2 * unit
        gate = acts_ref[:, at : at + unit].astype(jnp.float32)
        up = acts_ref[:, at + unit : at + 2 * unit].astype(jnp.float32)
        return gate, up

    rows = []
    for choice in range(2):
        gate, up = gate_and_up(choice)
        rows.append((gate * jax.nn.sigmoid(gate) * up).astype(jnp.bfloat16))
    placed = dot(table[...], jnp.concatenate(rows, axis=0), 1, 0)
    h_send[...] = placed.reshape(places, capacity, unit).astype(jnp.bfloat16)

    unsent = []

    def arrived(dst, at):
        pltpu.make_async_copy(dst, dst, recv_sem.at[at]).wait()

    def sent(src, at):
        pltpu.make_async_copy(src, src, send_sem.at[at]).wait()

    def to_experts(src, dst, at):
        def send(step, carry):
            peer = expert_peer(step)
            pltpu.make_async_remote_copy(
                src_ref=src.at[peer],
                dst_ref=dst.at[me],
                send_sem=send_sem.at[at],
                recv_sem=recv_sem.at[at],
                device_id={"expert": peer},
            ).start()
            return carry

        lax.fori_loop(1, places, send, 0)
        pltpu.make_async_copy(src.at[me], dst.at[me], recv_sem.at[at]).start()
        unsent.append((dst.at[pl.ds(0, places - 1)], at))

    def to_hidden(pick, dst, at):
        def send(step, carry):
            peer = hidden_peer(step)
            pltpu.make_async_remote_copy(
                src_ref=pick(peer),
                dst_ref=dst.at[mine],
                send_sem=send_sem.at[at],
                recv_sem=recv_sem.at[at],
                device_id={"hidden": peer},
            ).start()
            return carry

        lax.fori_loop(1, n_hidden, send, 0)
        pltpu.make_async_copy(pick(mine), dst.at[mine], recv_sem.at[at]).start()
        unsent.append((dst.at[pl.ds(0, n_hidden - 1)], at))

    rows = [
        (route_ref[choice : choice + 1, :] * gout_ref[...].astype(jnp.float32)).astype(jnp.bfloat16)
        for choice in range(2)
    ]
    placed = dot(table[...], jnp.concatenate(rows, axis=1), 1, 1)
    core = lax.rem(me, 2)
    span = g_recv.shape[2]
    rest = 2 * feat - span

    def paired(rows):
        rows = rows.reshape(places // 2, 2, capacity, feat)
        return jnp.concatenate([rows[:, 0], rows[:, 1]], axis=2).astype(jnp.bfloat16)

    def to_chips(src, dst, at, first=1, last=places // 2):
        def to_core(chip, side):
            if side == 0:
                part, target = src.at[chip, :, pl.ds(0, span)], dst.at[me]
            else:
                part, target = src.at[chip, :, pl.ds(span, rest)], dst.at[me, :, pl.ds(span - rest, rest)]
            return part, target

        def start(chip, side):
            part, target = to_core(chip, side)
            pltpu.make_async_remote_copy(
                src_ref=part,
                dst_ref=target,
                send_sem=send_sem.at[at + side],
                recv_sem=recv_sem.at[at],
                device_id={"expert": 2 * chip + side},
            ).start()

        def send(step, carry):
            chip = far_first(me // 2, step, places // 2)
            start(chip, 0)
            start(chip, 1)
            return carry

        lax.fori_loop(first, last, send, 0)
        if last == places // 2:
            for side in range(2):

                @pl.when(core == side)
                def _(side=side):
                    start(me // 2, 1 - side)
                    part, target = to_core(me // 2, side)
                    pltpu.make_async_copy(part, target, recv_sem.at[at]).start()

    def from_chips(dst, rows, at):
        def unpack(offset):
            return dst[:, :, offset : offset + feat].astype(jnp.float32).reshape(slots, feat).astype(jnp.bfloat16)

        seam = dst.at[:, :, pl.ds(span - LANES, LANES)]
        other = dst.at[:, :, pl.ds(0, LANES)]

        @pl.when(core == 0)
        def _():
            arrived(dst, at)
            if rest < span:
                pltpu.make_async_remote_copy(
                    src_ref=seam,
                    dst_ref=other,
                    send_sem=send_sem.at[at + 2],
                    recv_sem=recv_sem.at[at + 1],
                    device_id={"expert": me + 1},
                ).start()
            rows[...] = unpack(0)

        @pl.when(core == 1)
        def _():
            arrived(dst.at[:, :, pl.ds(span - rest, rest)], at)
            if rest < span:
                arrived(other, at + 1)
            rows[...] = unpack(span - feat)

    def chips_sent(dst, at):
        half = places // 2
        for side in range(2):

            @pl.when(core == side)
            def _(side=side):
                sent(dst.at[pl.ds(0, half - (side == 0))], at)
                sent(dst.at[pl.ds(0, half - (side == 1)), :, pl.ds(0, rest)], at + 1)

        if rest < span:

            @pl.when(core == 0)
            def _():
                sent(dst.at[:, :, pl.ds(0, LANES)], at + 2)

    g_send[...] = paired(placed)
    def send_blocks(product, src, dst, at):
        def send(step, carry):
            peer = hidden_peer(step)
            src[peer] = product(peer).astype(jnp.bfloat16)
            pltpu.make_async_remote_copy(
                src_ref=src.at[peer],
                dst_ref=dst.at[mine],
                send_sem=send_sem.at[at],
                recv_sem=recv_sem.at[at],
                device_id={"hidden": peer},
            ).start()
            return carry

        lax.fori_loop(1, n_hidden, send, 0)
        src[mine] = product(mine).astype(jnp.bfloat16)
        pltpu.make_async_copy(src.at[mine], dst.at[mine], recv_sem.at[at]).start()
        unsent.append((dst.at[pl.ds(0, n_hidden - 1)], at))

    pl.semaphore_wait(barrier, places + n_hidden - 2)
    def weight_window(peer):
        at = pl.multiple_of(peer * feat // LANES * LANES, LANES)
        return w_hbm.at[:, pl.ds(at, span)]

    to_hidden(weight_window, w_recv, 1)
    to_experts(h_send, h_recv, 0)
    to_chips(g_send, g_recv, GRADS)

    place = lax.broadcasted_iota(jnp.int32, (128, swap_ref.shape[1]), 0)
    left, right = swap_ref[0:1, :], swap_ref[1:2, :]
    trades = jnp.where(place == left, right, 0) + jnp.where(place == right, left, 0)
    trades = jnp.sum(trades, axis=1, keepdims=True)
    partner_row[...] = jnp.broadcast_to(trades, (128, 128)).T[0:1, :]
    table_copy = pltpu.make_async_copy(partner_row, partner_ref, local_sem.at[3])
    table_copy.start()

    arrived(h_recv, 0)
    h_own[...] = h_recv[...].astype(jnp.float32).reshape(slots, unit).astype(jnp.bfloat16)
    to_hidden(lambda peer: h_own, h_all, 3)
    arrived(w_recv, 1)
    shift = span - feat

    @pl.when(lax.rem(mine * feat, LANES) == 0)
    def _():
        w_all[...] = w_recv[:, :, :feat]

    @pl.when(lax.rem(mine * feat, LANES) != 0)
    def _():
        w_all[...] = w_recv[:, :, shift:]

    arrived(h_all, 3)
    h_cat = jnp.concatenate([h_all[block] for block in range(n_hidden)], axis=1)
    y_send[...] = paired(dot(h_cat, w_all[...].reshape(n_hidden * unit, feat), 1, 0))
    to_chips(y_send, y_recv, OUTPUTS, 1, places // 4)
    from_chips(g_recv, g_rows, GRADS)
    grads = g_rows[...]
    send_blocks(lambda block: dot(h_all[block], grads, 0, 0), gw_send, gw_recv, 5)
    to_chips(y_send, y_recv, OUTPUTS, places // 4, places // 2)

    arrived(gw_recv, 5)
    for load in loads:
        load.wait()

    def spare_seat(group):
        return stride - 1 - 2 * lax.rem(group, stride // 2)

    def past_spare(at, group):
        return (at + stride - spare_seat(group)) // stride

    my_group, my_seat = me // stride, lax.rem(me, stride)
    is_mid = my_seat != spare_seat(my_group)
    my_row = pl.multiple_of(my_group * ROWS, ROWS)
    my_col = (my_seat - past_spare(my_seat, my_group)) * COLS
    wide = COLS // PARTS

    def column_at(base, part):
        return pl.ds(pl.multiple_of(base + part * wide, wide), wide)

    def send_rows(group, part):
        at = pl.multiple_of(group * ROWS, ROWS)

        def send(col, carry):
            peer = group * stride + col + past_spare(col, group)
            chunk = u_here.at[pl.ds(at, ROWS), column_at(col * COLS, part)]

            @pl.when(peer == me)
            def _():
                pltpu.make_async_copy(chunk, u_mid.at[part, me], recv_sem.at[8 + part]).start()

            @pl.when(peer != me)
            def _():
                pltpu.make_async_remote_copy(
                    src_ref=chunk,
                    dst_ref=u_mid.at[part, me],
                    send_sem=send_sem.at[8 + part],
                    recv_sem=recv_sem.at[8 + part],
                    device_id={"expert": peer},
                ).start()

            return carry

        lax.fori_loop(0, col_groups, send, 0)

    def row_group(step):
        return far_first(me // stride, step, row_groups)

    def update_rows(step, carry):
        group = row_group(step)
        at = pl.multiple_of(group * ROWS, ROWS)
        for pair in range(n_hidden // 2):
            span = slice(pair * 2 * feat, (pair + 1) * 2 * feat)
            grad = jnp.concatenate(
                [
                    gw_recv[2 * pair, pl.ds(at, ROWS), :],
                    gw_recv[2 * pair + 1, pl.ds(at, ROWS), :],
                ],
                axis=1,
            ).astype(jnp.float32)
            first = m_here[pl.ds(at, ROWS), span].astype(jnp.float32)
            second = v_here[pl.ds(at, ROWS), span].astype(jnp.float32)
            first_new = first_decay * first + (1.0 - first_decay) * grad
            second_new = second_decay * second + (1.0 - second_decay) * grad * grad
            u_here[pl.ds(at, ROWS), span] = (
                first_new / (jnp.sqrt(second_new) + adam_epsilon)
            ).astype(jnp.bfloat16)
        send_rows(group, 0)
        return carry

    lax.fori_loop(1, row_groups + 1, update_rows, 0)
    send_blocks(lambda block: dot(grads, w_all[block], 1, 1), gh_send, gh_recv, 6)

    from_chips(y_recv, y_rows, OUTPUTS)
    back = y_rows[...]
    picked = dot(back, table[...], 0, 0)
    comb_ref[...] = (
        route_ref[0:1, :] * picked[:, :tok] + route_ref[1:2, :] * picked[:, tok:]
    ).astype(jnp.bfloat16)
    arrived(gh_recv, 6)
    total = gh_recv[0].astype(jnp.float32)
    for block in range(1, n_hidden):
        total = total + gh_recv[block].astype(jnp.float32)
    gr_send[...] = total.reshape(places, capacity, unit).astype(jnp.bfloat16)

    @pl.when(is_mid)
    def _():
        for part in range(PARTS):
            sent(u_mid.at[part, pl.ds(0, row_groups * col_groups - 1)], 8 + part)

    @pl.when(jnp.logical_not(is_mid))
    def _():
        for part in range(PARTS):
            sent(u_mid.at[part, pl.ds(0, row_groups * col_groups)], 8 + part)

    to_experts(gr_send, gr_recv, 7)
    table_copy.wait()

    @pl.when(is_mid)
    def _():
        for part in range(PARTS):
            arrived(u_mid.at[part], 8 + part)
            target = upd_hbm.at[pl.ds(my_row, ROWS), column_at(my_col, part)]

            def forward(step, carry, part=part, target=target):
                peer = expert_peer(step)
                u_out[part, peer] = u_mid[part, partner_ref[0, peer]]
                pltpu.make_async_remote_copy(
                    src_ref=u_out.at[part, peer],
                    dst_ref=target,
                    send_sem=send_sem.at[8 + PARTS],
                    recv_sem=recv_sem.at[8 + PARTS],
                    device_id={"expert": peer},
                ).start()
                return carry

            lax.fori_loop(1, places, forward, 0)
            u_out[part, me] = u_mid[part, partner_ref[0, me]]
            pltpu.make_async_copy(u_out.at[part, me], target, recv_sem.at[8 + PARTS]).start()

    arrived(gr_recv, 7)
    back = gr_recv[...].astype(jnp.float32).reshape(slots, unit).astype(jnp.bfloat16)
    picked = dot(table[...], back, 0, 0)
    for choice in range(2):
        gate, up = gate_and_up(choice)
        sig = jax.nn.sigmoid(gate)
        grad_hidden = picked[choice * tok : (choice + 1) * tok]
        at = choice * 2 * unit
        ggu_ref[:, at : at + unit] = (
            grad_hidden * up * sig * (1.0 + gate * (1.0 - sig))
        ).astype(jnp.bfloat16)
        ggu_ref[:, at + unit : at + 2 * unit] = (grad_hidden * (gate * sig)).astype(jnp.bfloat16)
    for src, at in unsent:
        sent(src, at)
    chips_sent(g_recv, GRADS)
    chips_sent(y_recv, OUTPUTS)

    arrived(upd_hbm, 8 + PARTS)

    @pl.when(is_mid)
    def _():
        for part in range(PARTS):
            sent(u_out.at[part, pl.ds(0, places - 1)], 8 + PARTS)


def local(
    swap_pairs,
    expert_ids,
    route_weights,
    gate_up,
    grad_out,
    down_weight,
    first_moment,
    second_moment,
):
    places = lax.axis_size("expert")
    n_hidden = lax.axis_size("hidden")
    tok, top = expert_ids.shape
    unit, depth = down_weight.shape[1:]
    feat = grad_out.shape[1]
    capacity = 2 * tok * top // places
    slots = places * capacity
    bf16 = jnp.bfloat16
    vmem = pl.BlockSpec(memory_space=pltpu.VMEM)
    anywhere = pl.BlockSpec(memory_space=pl.ANY)
    scratch = [
        ((n_hidden, unit, feat), bf16),
        ((unit, depth), bf16),
        ((unit, depth), bf16),
        ((slots, tok * top), bf16),
        ((places, capacity, unit), bf16),
        ((places, capacity, unit), bf16),
        ((places // 2, capacity, 2 * feat), bf16),
        ((places, capacity, -(-feat // LANES) * LANES), bf16),
        ((slots, feat), bf16),
        ((n_hidden, unit, -(-feat // LANES) * LANES), bf16),
        ((slots, unit), bf16),
        ((n_hidden, slots, unit), bf16),
        ((places // 2, capacity, 2 * feat), bf16),
        ((places, capacity, -(-feat // LANES) * LANES), bf16),
        ((slots, feat), bf16),
        ((n_hidden, unit, feat), bf16),
        ((n_hidden, unit, feat), bf16),
        ((n_hidden, slots, unit), bf16),
        ((n_hidden, slots, unit), bf16),
        ((places, capacity, unit), bf16),
        ((places, capacity, unit), bf16),
        ((unit, depth), bf16),
        ((PARTS, places, ROWS, COLS // PARTS), bf16),
        ((PARTS, places, ROWS, COLS // PARTS), bf16),
        ((1, 128), jnp.int32),
    ]
    combined, grads, update = pl.pallas_call(
        functools.partial(kernel, places, n_hidden, capacity),
        out_shape=(
            jax.ShapeDtypeStruct((feat, tok), bf16),
            jax.ShapeDtypeStruct((tok, top * 2 * unit), bf16),
            jax.ShapeDtypeStruct((unit, depth), bf16),
        ),
        in_specs=[vmem] * 5 + [anywhere] * 3,
        out_specs=(vmem, vmem, anywhere),
        scratch_shapes=[pltpu.VMEM(shape, kind) for shape, kind in scratch]
        + [
            pltpu.SMEM((1, 128), jnp.int32),
            pltpu.SemaphoreType.DMA((4,)),
            pltpu.SemaphoreType.DMA((20,)),
            pltpu.SemaphoreType.DMA((20,)),
        ],
        compiler_params=pltpu.CompilerParams(
            collective_id=0, has_side_effects=True, vmem_limit_bytes=VMEM_BYTES
        ),
    )(
        swap_pairs.T,
        expert_ids.T,
        route_weights.T,
        gate_up.reshape(tok, top * 2 * unit),
        grad_out.T,
        down_weight[0],
        first_moment[0],
        second_moment[0],
    )
    return combined.T, grads.reshape(tok, top, 2, unit), update[None]


def solution(mesh):
    placed = (
        P(),
        P("expert", None),
        P("expert", None),
        P("expert", None, None, "hidden"),
        P("expert", "hidden"),
        P("expert", "hidden", None),
        P("expert", "hidden", None),
        P("expert", "hidden", None),
    )
    return jax.shard_map(
        local,
        mesh=mesh,
        in_specs=placed,
        out_specs=(
            P("expert", "hidden"),
            P("expert", None, None, "hidden"),
            P("expert", "hidden", None),
        ),
        check_vma=False,
    )
```

```python
import functools

import jax
import jax.numpy as jnp
from jax import lax
from jax.experimental import pallas as pl
from jax.experimental.pallas import tpu as pltpu
from jax.sharding import PartitionSpec as P

first_decay = 0.9
second_decay = 0.95
adam_epsilon = 1e-08
ROWS = 16
COLS = 512
PARTS = 1
LANES = 128
GRADS = 12
OUTPUTS = 16
VMEM_BYTES = 52 * 1024 * 1024


def dot(a, b, contract_a, contract_b):
    return lax.dot_general(
        a, b, (((contract_a,), (contract_b,)), ((), ())), preferred_element_type=jnp.float32
    )


def kernel(
    places,
    n_hidden,
    capacity,
    swap_ref,
    ids_ref,
    route_ref,
    acts_ref,
    gout_ref,
    w_hbm,
    m_hbm,
    v_hbm,
    comb_ref,
    ggu_ref,
    upd_hbm,
    w_all,
    m_here,
    v_here,
    table,
    h_send,
    h_recv,
    g_send,
    g_recv,
    g_rows,
    w_recv,
    h_own,
    h_all,
    y_send,
    y_recv,
    y_rows,
    gw_send,
    gw_recv,
    gh_send,
    gh_recv,
    gr_send,
    gr_recv,
    u_here,
    u_mid,
    u_out,
    partner_row,
    partner_ref,
    local_sem,
    send_sem,
    recv_sem,
):
    me = lax.axis_index("expert")
    mine = lax.axis_index("hidden")
    tok = ids_ref.shape[1]
    count = 2 * tok
    slots = places * capacity
    unit = h_own.shape[1]
    feat = gout_ref.shape[0]
    row_groups = m_here.shape[0] // ROWS
    col_groups = m_here.shape[1] // COLS
    stride = places // row_groups

    def far_first(at, step, length):
        near = length - step
        half = (near + 1) // 2
        return lax.rem(at + half + (1 - lax.rem(near, 2)) * (length - 2 * half), length)

    def expert_peer(step):
        return far_first(me, step, places)

    def hidden_peer(step):
        return lax.rem(mine + step, n_hidden)

    barrier = pltpu.get_barrier_semaphore()

    def greet_expert(step, carry):
        pl.semaphore_signal(barrier, inc=1, device_id={"expert": expert_peer(step)})
        return carry

    def greet_hidden(step, carry):
        pl.semaphore_signal(barrier, inc=1, device_id={"hidden": hidden_peer(step)})
        return carry

    lax.fori_loop(1, places, greet_expert, 0)
    lax.fori_loop(1, n_hidden, greet_hidden, 0)

    loads = [
        pltpu.make_async_copy(src, dst, local_sem.at[at])
        for at, (src, dst) in enumerate(((m_hbm, m_here), (v_hbm, v_here)))
    ]
    for load in loads:
        load.start()

    ids = jnp.concatenate([ids_ref[0:1, :], ids_ref[1:2, :]], axis=1)
    hot = (lax.broadcasted_iota(jnp.int32, (places, count), 0) == ids).astype(jnp.float32)
    earlier = (
        lax.broadcasted_iota(jnp.int32, (count, count), 0)
        < lax.broadcasted_iota(jnp.int32, (count, count), 1)
    ).astype(jnp.bfloat16)
    before = dot(hot.astype(jnp.bfloat16), earlier, 1, 0)
    rank = jnp.sum(before * hot, axis=0, keepdims=True).astype(jnp.int32)
    slot = ids * capacity + rank
    table[...] = (lax.broadcasted_iota(jnp.int32, (slots, count), 0) == slot).astype(jnp.bfloat16)

    def picks(kind):
        row = lax.broadcasted_iota(jnp.int32, (count, 2 * count), 0)
        wanted = 4 * lax.rem(row, tok) + 2 * (row // tok) + kind
        return (lax.broadcasted_iota(jnp.int32, (count, 2 * count), 1) == wanted).astype(jnp.bfloat16)

    def gate_and_up():
        return dot(picks(0), acts_ref[...], 1, 0), dot(picks(1), acts_ref[...], 1, 0)

    gate, up = gate_and_up()
    hidden = (gate * jax.nn.sigmoid(gate) * up).astype(jnp.bfloat16)
    placed = dot(table[...], hidden, 1, 0)
    h_send[...] = placed.reshape(places, capacity, unit).astype(jnp.bfloat16)

    unsent = []

    def arrived(dst, at):
        pltpu.make_async_copy(dst, dst, recv_sem.at[at]).wait()

    def sent(src, at):
        pltpu.make_async_copy(src, src, send_sem.at[at]).wait()

    def to_experts(src, dst, at):
        def send(step, carry):
            peer = expert_peer(step)
            pltpu.make_async_remote_copy(
                src_ref=src.at[peer],
                dst_ref=dst.at[me],
                send_sem=send_sem.at[at],
                recv_sem=recv_sem.at[at],
                device_id={"expert": peer},
            ).start()
            return carry

        lax.fori_loop(1, places, send, 0)
        pltpu.make_async_copy(src.at[me], dst.at[me], recv_sem.at[at]).start()
        unsent.append((dst.at[pl.ds(0, places - 1)], at))

    def to_hidden(pick, dst, at):
        def send(step, carry):
            peer = hidden_peer(step)
            pltpu.make_async_remote_copy(
                src_ref=pick(peer),
                dst_ref=dst.at[mine],
                send_sem=send_sem.at[at],
                recv_sem=recv_sem.at[at],
                device_id={"hidden": peer},
            ).start()
            return carry

        lax.fori_loop(1, n_hidden, send, 0)
        pltpu.make_async_copy(pick(mine), dst.at[mine], recv_sem.at[at]).start()
        unsent.append((dst.at[pl.ds(0, n_hidden - 1)], at))

    rows = [
        (route_ref[choice : choice + 1, :] * gout_ref[...].astype(jnp.float32)).astype(jnp.bfloat16)
        for choice in range(2)
    ]
    placed = dot(table[...], jnp.concatenate(rows, axis=1), 1, 1)
    core = lax.rem(me, 2)
    span = g_recv.shape[2]
    rest = 2 * feat - span

    def paired(rows):
        rows = rows.reshape(places // 2, 2, capacity, feat)
        return jnp.concatenate([rows[:, 0], rows[:, 1]], axis=2).astype(jnp.bfloat16)

    def to_chips(src, dst, at, first=1, last=places // 2):
        def to_core(chip, side):
            if side == 0:
                part, target = src.at[chip, :, pl.ds(0, span)], dst.at[me]
            else:
                part, target = src.at[chip, :, pl.ds(span, rest)], dst.at[me, :, pl.ds(span - rest, rest)]
            return part, target

        def start(chip, side):
            part, target = to_core(chip, side)
            pltpu.make_async_remote_copy(
                src_ref=part,
                dst_ref=target,
                send_sem=send_sem.at[at + side],
                recv_sem=recv_sem.at[at],
                device_id={"expert": 2 * chip + side},
            ).start()

        def send(step, carry):
            chip = far_first(me // 2, step, places // 2)
            start(chip, 0)
            start(chip, 1)
            return carry

        lax.fori_loop(first, last, send, 0)
        if last == places // 2:
            for side in range(2):

                @pl.when(core == side)
                def _(side=side):
                    start(me // 2, 1 - side)
                    part, target = to_core(me // 2, side)
                    pltpu.make_async_copy(part, target, recv_sem.at[at]).start()

    def from_chips(dst, rows, at):
        def unpack(offset):
            return dst[:, :, offset : offset + feat].astype(jnp.float32).reshape(slots, feat).astype(jnp.bfloat16)

        seam = dst.at[:, :, pl.ds(span - LANES, LANES)]
        other = dst.at[:, :, pl.ds(0, LANES)]

        @pl.when(core == 0)
        def _():
            arrived(dst, at)
            if rest < span:
                pltpu.make_async_remote_copy(
                    src_ref=seam,
                    dst_ref=other,
                    send_sem=send_sem.at[at + 2],
                    recv_sem=recv_sem.at[at + 1],
                    device_id={"expert": me + 1},
                ).start()
            rows[...] = unpack(0)

        @pl.when(core == 1)
        def _():
            arrived(dst.at[:, :, pl.ds(span - rest, rest)], at)
            if rest < span:
                arrived(other, at + 1)
            rows[...] = unpack(span - feat)

    def chips_sent(dst, at):
        half = places // 2
        for side in range(2):

            @pl.when(core == side)
            def _(side=side):
                sent(dst.at[pl.ds(0, half - (side == 0))], at)
                sent(dst.at[pl.ds(0, half - (side == 1)), :, pl.ds(0, rest)], at + 1)

        if rest < span:

            @pl.when(core == 0)
            def _():
                sent(dst.at[:, :, pl.ds(0, LANES)], at + 2)

    g_send[...] = paired(placed)
    def send_blocks(product, src, dst, at):
        def send(step, carry):
            peer = hidden_peer(step)
            src[peer] = product(peer).astype(jnp.bfloat16)
            pltpu.make_async_remote_copy(
                src_ref=src.at[peer],
                dst_ref=dst.at[mine],
                send_sem=send_sem.at[at],
                recv_sem=recv_sem.at[at],
                device_id={"hidden": peer},
            ).start()
            return carry

        lax.fori_loop(1, n_hidden, send, 0)
        src[mine] = product(mine).astype(jnp.bfloat16)
        pltpu.make_async_copy(src.at[mine], dst.at[mine], recv_sem.at[at]).start()
        unsent.append((dst.at[pl.ds(0, n_hidden - 1)], at))

    pl.semaphore_wait(barrier, places + n_hidden - 2)
    def weight_window(peer):
        at = pl.multiple_of(peer * feat // LANES * LANES, LANES)
        return w_hbm.at[:, pl.ds(at, span)]

    to_hidden(weight_window, w_recv, 1)
    to_experts(h_send, h_recv, 0)
    to_chips(g_send, g_recv, GRADS)

    place = lax.broadcasted_iota(jnp.int32, (128, swap_ref.shape[1]), 0)
    left, right = swap_ref[0:1, :], swap_ref[1:2, :]
    trades = jnp.where(place == left, right, 0) + jnp.where(place == right, left, 0)
    trades = jnp.sum(trades, axis=1, keepdims=True)
    partner_row[...] = jnp.broadcast_to(trades, (128, 128)).T[0:1, :]
    table_copy = pltpu.make_async_copy(partner_row, partner_ref, local_sem.at[3])
    table_copy.start()

    arrived(h_recv, 0)
    h_own[...] = h_recv[...].astype(jnp.float32).reshape(slots, unit).astype(jnp.bfloat16)
    to_hidden(lambda peer: h_own, h_all, 3)
    arrived(w_recv, 1)
    shift = span - feat

    @pl.when(lax.rem(mine * feat, LANES) == 0)
    def _():
        w_all[...] = w_recv[:, :, :feat]

    @pl.when(lax.rem(mine * feat, LANES) != 0)
    def _():
        w_all[...] = w_recv[:, :, shift:]

    arrived(h_all, 3)
    h_cat = jnp.concatenate([h_all[block] for block in range(n_hidden)], axis=1)
    y_send[...] = paired(dot(h_cat, w_all[...].reshape(n_hidden * unit, feat), 1, 0))
    early = max(1, places // 8)
    to_chips(y_send, y_recv, OUTPUTS, 1, early)
    from_chips(g_recv, g_rows, GRADS)
    grads = g_rows[...]
    send_blocks(lambda block: dot(h_all[block], grads, 0, 0), gw_send, gw_recv, 5)
    to_chips(y_send, y_recv, OUTPUTS, early, places // 2)

    arrived(gw_recv, 5)
    for load in loads:
        load.wait()

    def spare_seat(group):
        return stride - 1 - 2 * lax.rem(group, stride // 2)

    def past_spare(at, group):
        return (at + stride - spare_seat(group)) // stride

    my_group, my_seat = me // stride, lax.rem(me, stride)
    is_mid = my_seat != spare_seat(my_group)
    my_row = pl.multiple_of(my_group * ROWS, ROWS)
    my_col = (my_seat - past_spare(my_seat, my_group)) * COLS
    wide = COLS // PARTS

    def column_at(base, part):
        return pl.ds(pl.multiple_of(base + part * wide, wide), wide)

    def send_rows(group, part):
        at = pl.multiple_of(group * ROWS, ROWS)

        def send(col, carry):
            peer = group * stride + col + past_spare(col, group)
            chunk = u_here.at[pl.ds(at, ROWS), column_at(col * COLS, part)]

            @pl.when(peer == me)
            def _():
                pltpu.make_async_copy(chunk, u_mid.at[part, me], recv_sem.at[8 + part]).start()

            @pl.when(peer != me)
            def _():
                pltpu.make_async_remote_copy(
                    src_ref=chunk,
                    dst_ref=u_mid.at[part, me],
                    send_sem=send_sem.at[8 + part],
                    recv_sem=recv_sem.at[8 + part],
                    device_id={"expert": peer},
                ).start()

            return carry

        lax.fori_loop(0, col_groups, send, 0)

    def row_group(step):
        return far_first(me // stride, step, row_groups)

    def update_rows(step, carry):
        group = row_group(step)
        at = pl.multiple_of(group * ROWS, ROWS)
        for pair in range(n_hidden // 2):
            span = slice(pair * 2 * feat, (pair + 1) * 2 * feat)
            grad = jnp.concatenate(
                [
                    gw_recv[2 * pair, pl.ds(at, ROWS), :],
                    gw_recv[2 * pair + 1, pl.ds(at, ROWS), :],
                ],
                axis=1,
            ).astype(jnp.float32)
            first = m_here[pl.ds(at, ROWS), span].astype(jnp.float32)
            second = v_here[pl.ds(at, ROWS), span].astype(jnp.float32)
            first_new = first_decay * first + (1.0 - first_decay) * grad
            second_new = second_decay * second + (1.0 - second_decay) * grad * grad
            u_here[pl.ds(at, ROWS), span] = (
                first_new / (jnp.sqrt(second_new) + adam_epsilon)
            ).astype(jnp.bfloat16)
        send_rows(group, 0)
        return carry

    lax.fori_loop(1, row_groups + 1, update_rows, 0)
    send_blocks(lambda block: dot(grads, w_all[block], 1, 1), gh_send, gh_recv, 6)

    from_chips(y_recv, y_rows, OUTPUTS)
    back = y_rows[...]
    picked = dot(back, table[...], 0, 0)
    comb_ref[...] = (
        route_ref[0:1, :] * picked[:, :tok] + route_ref[1:2, :] * picked[:, tok:]
    ).astype(jnp.bfloat16)
    arrived(gh_recv, 6)
    total = gh_recv[0].astype(jnp.float32)
    for block in range(1, n_hidden):
        total = total + gh_recv[block].astype(jnp.float32)
    gr_send[...] = total.reshape(places, capacity, unit).astype(jnp.bfloat16)

    @pl.when(is_mid)
    def _():
        for part in range(PARTS):
            sent(u_mid.at[part, pl.ds(0, row_groups * col_groups - 1)], 8 + part)

    @pl.when(jnp.logical_not(is_mid))
    def _():
        for part in range(PARTS):
            sent(u_mid.at[part, pl.ds(0, row_groups * col_groups)], 8 + part)

    to_experts(gr_send, gr_recv, 7)
    table_copy.wait()

    @pl.when(is_mid)
    def _():
        for part in range(PARTS):
            arrived(u_mid.at[part], 8 + part)
            target = upd_hbm.at[pl.ds(my_row, ROWS), column_at(my_col, part)]

            def forward(step, carry, part=part, target=target):
                peer = expert_peer(step)
                u_out[part, peer] = u_mid[part, partner_ref[0, peer]]
                pltpu.make_async_remote_copy(
                    src_ref=u_out.at[part, peer],
                    dst_ref=target,
                    send_sem=send_sem.at[8 + PARTS],
                    recv_sem=recv_sem.at[8 + PARTS],
                    device_id={"expert": peer},
                ).start()
                return carry

            lax.fori_loop(1, places, forward, 0)
            u_out[part, me] = u_mid[part, partner_ref[0, me]]
            pltpu.make_async_copy(u_out.at[part, me], target, recv_sem.at[8 + PARTS]).start()

    arrived(gr_recv, 7)
    back = gr_recv[...].astype(jnp.float32).reshape(slots, unit).astype(jnp.bfloat16)
    grad_hidden = dot(table[...], back, 0, 0)
    gate, up = gate_and_up()
    sig = jax.nn.sigmoid(gate)
    grad_gate = (grad_hidden * up * sig * (1.0 + gate * (1.0 - sig))).astype(jnp.bfloat16)
    grad_up = (grad_hidden * (gate * sig)).astype(jnp.bfloat16)
    ggu_ref[...] = (dot(picks(0), grad_gate, 0, 0) + dot(picks(1), grad_up, 0, 0)).astype(
        jnp.bfloat16
    )
    for src, at in unsent:
        sent(src, at)
    chips_sent(g_recv, GRADS)
    chips_sent(y_recv, OUTPUTS)

    arrived(upd_hbm, 8 + PARTS)

    @pl.when(is_mid)
    def _():
        for part in range(PARTS):
            sent(u_out.at[part, pl.ds(0, places - 1)], 8 + PARTS)


def local(
    swap_pairs,
    expert_ids,
    route_weights,
    gate_up,
    grad_out,
    down_weight,
    first_moment,
    second_moment,
):
    places = lax.axis_size("expert")
    n_hidden = lax.axis_size("hidden")
    tok, top = expert_ids.shape
    unit, depth = down_weight.shape[1:]
    feat = grad_out.shape[1]
    capacity = 2 * tok * top // places
    slots = places * capacity
    bf16 = jnp.bfloat16
    vmem = pl.BlockSpec(memory_space=pltpu.VMEM)
    anywhere = pl.BlockSpec(memory_space=pl.ANY)
    scratch = [
        ((n_hidden, unit, feat), bf16),
        ((unit, depth), bf16),
        ((unit, depth), bf16),
        ((slots, tok * top), bf16),
        ((places, capacity, unit), bf16),
        ((places, capacity, unit), bf16),
        ((places // 2, capacity, 2 * feat), bf16),
        ((places, capacity, -(-feat // LANES) * LANES), bf16),
        ((slots, feat), bf16),
        ((n_hidden, unit, -(-feat // LANES) * LANES), bf16),
        ((slots, unit), bf16),
        ((n_hidden, slots, unit), bf16),
        ((places // 2, capacity, 2 * feat), bf16),
        ((places, capacity, -(-feat // LANES) * LANES), bf16),
        ((slots, feat), bf16),
        ((n_hidden, unit, feat), bf16),
        ((n_hidden, unit, feat), bf16),
        ((n_hidden, slots, unit), bf16),
        ((n_hidden, slots, unit), bf16),
        ((places, capacity, unit), bf16),
        ((places, capacity, unit), bf16),
        ((unit, depth), bf16),
        ((PARTS, places, ROWS, COLS // PARTS), bf16),
        ((PARTS, places, ROWS, COLS // PARTS), bf16),
        ((1, 128), jnp.int32),
    ]
    combined, grads, update = pl.pallas_call(
        functools.partial(kernel, places, n_hidden, capacity),
        out_shape=(
            jax.ShapeDtypeStruct((feat, tok), bf16),
            jax.ShapeDtypeStruct((tok * top * 2, unit), bf16),
            jax.ShapeDtypeStruct((unit, depth), bf16),
        ),
        in_specs=[vmem] * 5 + [anywhere] * 3,
        out_specs=(vmem, vmem, anywhere),
        scratch_shapes=[pltpu.VMEM(shape, kind) for shape, kind in scratch]
        + [
            pltpu.SMEM((1, 128), jnp.int32),
            pltpu.SemaphoreType.DMA((4,)),
            pltpu.SemaphoreType.DMA((20,)),
            pltpu.SemaphoreType.DMA((20,)),
        ],
        compiler_params=pltpu.CompilerParams(
            collective_id=0, has_side_effects=True, vmem_limit_bytes=VMEM_BYTES
        ),
    )(
        swap_pairs.T,
        expert_ids.T,
        route_weights.T,
        gate_up.reshape(tok * top * 2, unit),
        grad_out.T,
        down_weight[0],
        first_moment[0],
        second_moment[0],
    )
    return combined.T, grads.reshape(tok, top, 2, unit), update[None]


def solution(mesh):
    placed = (
        P(),
        P("expert", None),
        P("expert", None),
        P("expert", None, None, "hidden"),
        P("expert", "hidden"),
        P("expert", "hidden", None),
        P("expert", "hidden", None),
        P("expert", "hidden", None),
    )
    return jax.shard_map(
        local,
        mesh=mesh,
        in_specs=placed,
        out_specs=(
            P("expert", "hidden"),
            P("expert", None, None, "hidden"),
            P("expert", "hidden", None),
        ),
        check_vma=False,
    )
```

```python
import functools

import jax
import jax.numpy as jnp
from jax import lax
from jax.experimental import pallas as pl
from jax.experimental.pallas import tpu as pltpu
from jax.sharding import PartitionSpec as P

first_decay = 0.9
second_decay = 0.95
adam_epsilon = 1e-08
ROWS = 16
COLS = 512
PARTS = 1
LANES = 128
GRADS = 12
OUTPUTS = 16
VMEM_BYTES = 52 * 1024 * 1024


def dot(a, b, contract_a, contract_b):
    return lax.dot_general(
        a, b, (((contract_a,), (contract_b,)), ((), ())), preferred_element_type=jnp.float32
    )


def kernel(
    places,
    n_hidden,
    capacity,
    swap_ref,
    ids_ref,
    route_ref,
    acts_ref,
    gout_ref,
    w_hbm,
    m_hbm,
    v_hbm,
    comb_ref,
    ggu_ref,
    upd_hbm,
    w_all,
    m_here,
    v_here,
    table,
    h_send,
    h_recv,
    g_send,
    g_recv,
    g_rows,
    w_recv,
    h_own,
    h_all,
    y_send,
    y_recv,
    y_rows,
    gw_send,
    gw_recv,
    gh_send,
    gh_recv,
    gr_send,
    gr_recv,
    u_here,
    u_mid,
    u_out,
    partner_row,
    partner_ref,
    local_sem,
    send_sem,
    recv_sem,
):
    me = lax.axis_index("expert")
    mine = lax.axis_index("hidden")
    tok = ids_ref.shape[1]
    count = 2 * tok
    slots = places * capacity
    unit = h_own.shape[1]
    feat = gout_ref.shape[0]
    row_groups = m_here.shape[0] // ROWS
    col_groups = m_here.shape[1] // COLS
    stride = places // row_groups

    def far_first(at, step, length):
        near = length - step
        half = (near + 1) // 2
        return lax.rem(at + half + (1 - lax.rem(near, 2)) * (length - 2 * half), length)

    def expert_peer(step):
        return far_first(me, step, places)

    def hidden_peer(step):
        return lax.rem(mine + step, n_hidden)

    barrier = pltpu.get_barrier_semaphore()

    def greet_expert(step, carry):
        pl.semaphore_signal(barrier, inc=1, device_id={"expert": expert_peer(step)})
        return carry

    def greet_hidden(step, carry):
        pl.semaphore_signal(barrier, inc=1, device_id={"hidden": hidden_peer(step)})
        return carry

    lax.fori_loop(1, places, greet_expert, 0)
    lax.fori_loop(1, n_hidden, greet_hidden, 0)

    loads = [
        pltpu.make_async_copy(src, dst, local_sem.at[at])
        for at, (src, dst) in enumerate(((m_hbm, m_here), (v_hbm, v_here)))
    ]
    for load in loads:
        load.start()

    ids = jnp.concatenate([ids_ref[0:1, :], ids_ref[1:2, :]], axis=1)
    hot = (lax.broadcasted_iota(jnp.int32, (places, count), 0) == ids).astype(jnp.float32)
    earlier = (
        lax.broadcasted_iota(jnp.int32, (count, count), 0)
        < lax.broadcasted_iota(jnp.int32, (count, count), 1)
    ).astype(jnp.bfloat16)
    before = dot(hot.astype(jnp.bfloat16), earlier, 1, 0)
    rank = jnp.sum(before * hot, axis=0, keepdims=True).astype(jnp.int32)
    slot = ids * capacity + rank
    table[...] = (lax.broadcasted_iota(jnp.int32, (slots, count), 0) == slot).astype(jnp.bfloat16)

    def gate_and_up(choice):
        at = choice * 2 * unit
        gate = acts_ref[:, at : at + unit].astype(jnp.float32)
        up = acts_ref[:, at + unit : at + 2 * unit].astype(jnp.float32)
        return gate, up

    rows = []
    for choice in range(2):
        gate, up = gate_and_up(choice)
        rows.append((gate * jax.nn.sigmoid(gate) * up).astype(jnp.bfloat16))
    placed = dot(table[...], jnp.concatenate(rows, axis=0), 1, 0)
    h_send[...] = placed.reshape(places, capacity, unit).astype(jnp.bfloat16)

    unsent = []

    def arrived(dst, at):
        pltpu.make_async_copy(dst, dst, recv_sem.at[at]).wait()

    def sent(src, at):
        pltpu.make_async_copy(src, src, send_sem.at[at]).wait()

    def to_experts(src, dst, at):
        def send(step, carry):
            peer = expert_peer(step)
            pltpu.make_async_remote_copy(
                src_ref=src.at[peer],
                dst_ref=dst.at[me],
                send_sem=send_sem.at[at],
                recv_sem=recv_sem.at[at],
                device_id={"expert": peer},
            ).start()
            return carry

        lax.fori_loop(1, places, send, 0)
        pltpu.make_async_copy(src.at[me], dst.at[me], recv_sem.at[at]).start()
        unsent.append((dst.at[pl.ds(0, places - 1)], at))

    def to_hidden(pick, dst, at):
        def send(step, carry):
            peer = hidden_peer(step)
            pltpu.make_async_remote_copy(
                src_ref=pick(peer),
                dst_ref=dst.at[mine],
                send_sem=send_sem.at[at],
                recv_sem=recv_sem.at[at],
                device_id={"hidden": peer},
            ).start()
            return carry

        lax.fori_loop(1, n_hidden, send, 0)
        pltpu.make_async_copy(pick(mine), dst.at[mine], recv_sem.at[at]).start()
        unsent.append((dst.at[pl.ds(0, n_hidden - 1)], at))

    rows = [
        (route_ref[choice : choice + 1, :] * gout_ref[...].astype(jnp.float32)).astype(jnp.bfloat16)
        for choice in range(2)
    ]
    placed = dot(table[...], jnp.concatenate(rows, axis=1), 1, 1)
    core = lax.rem(me, 2)
    span = g_recv.shape[2]
    rest = 2 * feat - span

    def paired(rows):
        rows = rows.reshape(places // 2, 2, capacity, feat)
        return jnp.concatenate([rows[:, 0], rows[:, 1]], axis=2).astype(jnp.bfloat16)

    def to_chips(src, dst, at, first=1, last=places // 2):
        def to_core(chip, side):
            if side == 0:
                part, target = src.at[chip, :, pl.ds(0, span)], dst.at[me]
            else:
                part, target = src.at[chip, :, pl.ds(span, rest)], dst.at[me, :, pl.ds(span - rest, rest)]
            return part, target

        def start(chip, side):
            part, target = to_core(chip, side)
            pltpu.make_async_remote_copy(
                src_ref=part,
                dst_ref=target,
                send_sem=send_sem.at[at + side],
                recv_sem=recv_sem.at[at],
                device_id={"expert": 2 * chip + side},
            ).start()

        def send(step, carry):
            chip = far_first(me // 2, step, places // 2)
            start(chip, 0)
            start(chip, 1)
            return carry

        lax.fori_loop(first, last, send, 0)
        if last == places // 2:
            for side in range(2):

                @pl.when(core == side)
                def _(side=side):
                    start(me // 2, 1 - side)
                    part, target = to_core(me // 2, side)
                    pltpu.make_async_copy(part, target, recv_sem.at[at]).start()

    def from_chips(dst, rows, at):
        def unpack(offset):
            return dst[:, :, offset : offset + feat].astype(jnp.float32).reshape(slots, feat).astype(jnp.bfloat16)

        seam = dst.at[:, :, pl.ds(span - LANES, LANES)]
        other = dst.at[:, :, pl.ds(0, LANES)]

        @pl.when(core == 0)
        def _():
            arrived(dst, at)
            if rest < span:
                pltpu.make_async_remote_copy(
                    src_ref=seam,
                    dst_ref=other,
                    send_sem=send_sem.at[at + 2],
                    recv_sem=recv_sem.at[at + 1],
                    device_id={"expert": me + 1},
                ).start()
            rows[...] = unpack(0)

        @pl.when(core == 1)
        def _():
            arrived(dst.at[:, :, pl.ds(span - rest, rest)], at)
            if rest < span:
                arrived(other, at + 1)
            rows[...] = unpack(span - feat)

    def chips_sent(dst, at):
        half = places // 2
        for side in range(2):

            @pl.when(core == side)
            def _(side=side):
                sent(dst.at[pl.ds(0, half - (side == 0))], at)
                sent(dst.at[pl.ds(0, half - (side == 1)), :, pl.ds(0, rest)], at + 1)

        if rest < span:

            @pl.when(core == 0)
            def _():
                sent(dst.at[:, :, pl.ds(0, LANES)], at + 2)

    g_send[...] = paired(placed)
    def send_blocks(product, src, dst, at):
        def send(step, carry):
            peer = hidden_peer(step)
            src[peer] = product(peer).astype(jnp.bfloat16)
            pltpu.make_async_remote_copy(
                src_ref=src.at[peer],
                dst_ref=dst.at[mine],
                send_sem=send_sem.at[at],
                recv_sem=recv_sem.at[at],
                device_id={"hidden": peer},
            ).start()
            return carry

        lax.fori_loop(1, n_hidden, send, 0)
        src[mine] = product(mine).astype(jnp.bfloat16)
        pltpu.make_async_copy(src.at[mine], dst.at[mine], recv_sem.at[at]).start()
        unsent.append((dst.at[pl.ds(0, n_hidden - 1)], at))

    pl.semaphore_wait(barrier, places + n_hidden - 2)
    def weight_window(peer):
        at = pl.multiple_of(peer * feat // LANES * LANES, LANES)
        return w_hbm.at[:, pl.ds(at, span)]

    to_hidden(weight_window, w_recv, 1)
    to_experts(h_send, h_recv, 0)
    to_chips(g_send, g_recv, GRADS)

    place = lax.broadcasted_iota(jnp.int32, (128, swap_ref.shape[1]), 0)
    left, right = swap_ref[0:1, :], swap_ref[1:2, :]
    trades = jnp.where(place == left, right, 0) + jnp.where(place == right, left, 0)
    trades = jnp.sum(trades, axis=1, keepdims=True)
    partner_row[...] = jnp.broadcast_to(trades, (128, 128)).T[0:1, :]
    table_copy = pltpu.make_async_copy(partner_row, partner_ref, local_sem.at[3])
    table_copy.start()

    arrived(h_recv, 0)
    h_own[...] = h_recv[...].astype(jnp.float32).reshape(slots, unit).astype(jnp.bfloat16)
    to_hidden(lambda peer: h_own, h_all, 3)
    arrived(w_recv, 1)
    shift = span - feat

    @pl.when(lax.rem(mine * feat, LANES) == 0)
    def _():
        w_all[...] = w_recv[:, :, :feat]

    @pl.when(lax.rem(mine * feat, LANES) != 0)
    def _():
        w_all[...] = w_recv[:, :, shift:]

    arrived(h_all, 3)
    h_cat = jnp.concatenate([h_all[block] for block in range(n_hidden)], axis=1)
    y_send[...] = paired(dot(h_cat, w_all[...].reshape(n_hidden * unit, feat), 1, 0))
    to_chips(y_send, y_recv, OUTPUTS, 1, places // 4)
    from_chips(g_recv, g_rows, GRADS)
    grads = g_rows[...]
    send_blocks(lambda block: dot(h_all[block], grads, 0, 0), gw_send, gw_recv, 5)
    to_chips(y_send, y_recv, OUTPUTS, places // 4, places // 2)

    arrived(gw_recv, 5)
    for load in loads:
        load.wait()

    def spare_seat(group):
        return stride - 1 - 2 * lax.rem(group, stride // 2)

    def past_spare(at, group):
        return (at + stride - spare_seat(group)) // stride

    my_group, my_seat = me // stride, lax.rem(me, stride)
    is_mid = my_seat != spare_seat(my_group)
    my_row = pl.multiple_of(my_group * ROWS, ROWS)
    my_col = (my_seat - past_spare(my_seat, my_group)) * COLS
    wide = COLS // PARTS

    def column_at(base, part):
        return pl.ds(pl.multiple_of(base + part * wide, wide), wide)

    def send_rows(group, part):
        at = pl.multiple_of(group * ROWS, ROWS)

        def send(col, carry):
            peer = group * stride + col + past_spare(col, group)
            chunk = u_here.at[pl.ds(at, ROWS), column_at(col * COLS, part)]

            @pl.when(peer == me)
            def _():
                pltpu.make_async_copy(chunk, u_mid.at[part, me], recv_sem.at[8 + part]).start()

            @pl.when(peer != me)
            def _():
                pltpu.make_async_remote_copy(
                    src_ref=chunk,
                    dst_ref=u_mid.at[part, me],
                    send_sem=send_sem.at[8 + part],
                    recv_sem=recv_sem.at[8 + part],
                    device_id={"expert": peer},
                ).start()

            return carry

        lax.fori_loop(0, col_groups, send, 0)

    def row_group(step):
        return far_first(me // stride, step, row_groups)

    def update_rows(step, carry):
        group = row_group(step)
        at = pl.multiple_of(group * ROWS, ROWS)
        for pair in range(n_hidden // 2):
            span = slice(pair * 2 * feat, (pair + 1) * 2 * feat)
            grad = jnp.concatenate(
                [
                    gw_recv[2 * pair, pl.ds(at, ROWS), :],
                    gw_recv[2 * pair + 1, pl.ds(at, ROWS), :],
                ],
                axis=1,
            ).astype(jnp.float32)
            first = m_here[pl.ds(at, ROWS), span].astype(jnp.float32)
            second = v_here[pl.ds(at, ROWS), span].astype(jnp.float32)
            first_new = first_decay * first + (1.0 - first_decay) * grad
            second_new = second_decay * second + (1.0 - second_decay) * grad * grad
            u_here[pl.ds(at, ROWS), span] = (
                first_new / (jnp.sqrt(second_new) + adam_epsilon)
            ).astype(jnp.bfloat16)
        send_rows(group, 0)
        return carry

    lax.fori_loop(1, row_groups + 1, update_rows, 0)
    send_blocks(lambda block: dot(grads, w_all[block], 1, 1), gh_send, gh_recv, 6)

    from_chips(y_recv, y_rows, OUTPUTS)
    back = y_rows[...]
    picked = dot(back, table[...], 0, 0)
    comb_ref[...] = (
        route_ref[0:1, :] * picked[:, :tok] + route_ref[1:2, :] * picked[:, tok:]
    ).astype(jnp.bfloat16)
    arrived(gh_recv, 6)
    total = gh_recv[0].astype(jnp.float32)
    for block in range(1, n_hidden):
        total = total + gh_recv[block].astype(jnp.float32)
    gr_send[...] = total.reshape(places, capacity, unit).astype(jnp.bfloat16)

    @pl.when(is_mid)
    def _():
        for part in range(PARTS):
            sent(u_mid.at[part, pl.ds(0, row_groups * col_groups - 1)], 8 + part)

    @pl.when(jnp.logical_not(is_mid))
    def _():
        for part in range(PARTS):
            sent(u_mid.at[part, pl.ds(0, row_groups * col_groups)], 8 + part)

    to_experts(gr_send, gr_recv, 7)
    table_copy.wait()

    @pl.when(is_mid)
    def _():
        for part in range(PARTS):
            arrived(u_mid.at[part], 8 + part)
            target = upd_hbm.at[pl.ds(my_row, ROWS), column_at(my_col, part)]

            def forward(step, carry, part=part, target=target):
                peer = expert_peer(step)
                u_out[part, peer] = u_mid[part, partner_ref[0, peer]]
                pltpu.make_async_remote_copy(
                    src_ref=u_out.at[part, peer],
                    dst_ref=target,
                    send_sem=send_sem.at[8 + PARTS],
                    recv_sem=recv_sem.at[8 + PARTS],
                    device_id={"expert": peer},
                ).start()
                return carry

            lax.fori_loop(1, places, forward, 0)
            u_out[part, me] = u_mid[part, partner_ref[0, me]]
            pltpu.make_async_copy(u_out.at[part, me], target, recv_sem.at[8 + PARTS]).start()

    arrived(gr_recv, 7)
    back = gr_recv[...].astype(jnp.float32).reshape(slots, unit).astype(jnp.bfloat16)
    picked = dot(table[...], back, 0, 0)
    row = lax.broadcasted_iota(jnp.int32, (count, 2 * count), 0)
    column = lax.broadcasted_iota(jnp.int32, (count, 2 * count), 1)
    wanted = 4 * lax.rem(row, tok) + 2 * (row // tok)
    rows = [[], []]
    for choice in range(2):
        gate, up = gate_and_up(choice)
        sig = jax.nn.sigmoid(gate)
        grad_hidden = picked[choice * tok : (choice + 1) * tok]
        rows[0].append(
            (grad_hidden * up * sig * (1.0 + gate * (1.0 - sig))).astype(jnp.bfloat16)
        )
        rows[1].append((grad_hidden * (gate * sig)).astype(jnp.bfloat16))
    spread = [
        dot((column == wanted + kind).astype(jnp.bfloat16), jnp.concatenate(rows[kind], axis=0), 0, 0)
        for kind in range(2)
    ]
    ggu_ref[...] = (spread[0] + spread[1]).astype(jnp.bfloat16)
    for src, at in unsent:
        sent(src, at)
    chips_sent(g_recv, GRADS)
    chips_sent(y_recv, OUTPUTS)

    arrived(upd_hbm, 8 + PARTS)

    @pl.when(is_mid)
    def _():
        for part in range(PARTS):
            sent(u_out.at[part, pl.ds(0, places - 1)], 8 + PARTS)


def hand_out(*refs):
    sources, targets, sem = refs[:3], refs[3:6], refs[6]
    copies = [
        pltpu.make_async_copy(sources[at], targets[at], sem.at[at]) for at in (2, 0, 1)
    ]
    for copy in copies:
        copy.start()
    for copy in copies:
        copy.wait()


def local(
    swap_pairs,
    expert_ids,
    route_weights,
    gate_up,
    grad_out,
    down_weight,
    first_moment,
    second_moment,
):
    places = lax.axis_size("expert")
    n_hidden = lax.axis_size("hidden")
    tok, top = expert_ids.shape
    unit, depth = down_weight.shape[1:]
    feat = grad_out.shape[1]
    capacity = 2 * tok * top // places
    slots = places * capacity
    bf16 = jnp.bfloat16
    vmem = pl.BlockSpec(memory_space=pltpu.VMEM)
    anywhere = pl.BlockSpec(memory_space=pl.ANY)
    scratch = [
        ((n_hidden, unit, feat), bf16),
        ((unit, depth), bf16),
        ((unit, depth), bf16),
        ((slots, tok * top), bf16),
        ((places, capacity, unit), bf16),
        ((places, capacity, unit), bf16),
        ((places // 2, capacity, 2 * feat), bf16),
        ((places, capacity, -(-feat // LANES) * LANES), bf16),
        ((slots, feat), bf16),
        ((n_hidden, unit, -(-feat // LANES) * LANES), bf16),
        ((slots, unit), bf16),
        ((n_hidden, slots, unit), bf16),
        ((places // 2, capacity, 2 * feat), bf16),
        ((places, capacity, -(-feat // LANES) * LANES), bf16),
        ((slots, feat), bf16),
        ((n_hidden, unit, feat), bf16),
        ((n_hidden, unit, feat), bf16),
        ((n_hidden, slots, unit), bf16),
        ((n_hidden, slots, unit), bf16),
        ((places, capacity, unit), bf16),
        ((places, capacity, unit), bf16),
        ((unit, depth), bf16),
        ((PARTS, places, ROWS, COLS // PARTS), bf16),
        ((PARTS, places, ROWS, COLS // PARTS), bf16),
        ((1, 128), jnp.int32),
    ]
    combined, grads, update = pl.pallas_call(
        functools.partial(kernel, places, n_hidden, capacity),
        out_shape=(
            jax.ShapeDtypeStruct((feat, tok), bf16),
            jax.ShapeDtypeStruct((tok * top * 2, unit), bf16),
            jax.ShapeDtypeStruct((unit, depth), bf16),
        ),
        in_specs=[vmem] * 5 + [anywhere] * 3,
        out_specs=(vmem, vmem, anywhere),
        scratch_shapes=[pltpu.VMEM(shape, kind) for shape, kind in scratch]
        + [
            pltpu.SMEM((1, 128), jnp.int32),
            pltpu.SemaphoreType.DMA((4,)),
            pltpu.SemaphoreType.DMA((20,)),
            pltpu.SemaphoreType.DMA((20,)),
        ],
        compiler_params=pltpu.CompilerParams(
            collective_id=0, has_side_effects=True, vmem_limit_bytes=VMEM_BYTES
        ),
    )(
        swap_pairs.T,
        expert_ids.T,
        route_weights.T,
        gate_up.reshape(tok, top * 2 * unit),
        grad_out.T,
        down_weight[0],
        first_moment[0],
        second_moment[0],
    )
    results = (combined, grads, update)
    combined, grads, update = pl.pallas_call(
        hand_out,
        out_shape=tuple(jax.ShapeDtypeStruct(out.shape, out.dtype) for out in results),
        in_specs=[anywhere] * 3,
        out_specs=(anywhere,) * 3,
        scratch_shapes=[pltpu.SemaphoreType.DMA((3,))],
        compiler_params=pltpu.CompilerParams(vmem_limit_bytes=VMEM_BYTES),
    )(*results)
    return combined.T, grads.reshape(tok, top, 2, unit), update[None]


def solution(mesh):
    placed = (
        P(),
        P("expert", None),
        P("expert", None),
        P("expert", None, None, "hidden"),
        P("expert", "hidden"),
        P("expert", "hidden", None),
        P("expert", "hidden", None),
        P("expert", "hidden", None),
    )
    return jax.shard_map(
        local,
        mesh=mesh,
        in_specs=placed,
        out_specs=(
            P("expert", "hidden"),
            P("expert", None, None, "hidden"),
            P("expert", "hidden", None),
        ),
        check_vma=False,
    )
```

```python
import functools

import jax
import jax.numpy as jnp
from jax import lax
from jax.experimental import pallas as pl
from jax.experimental.pallas import tpu as pltpu
from jax.sharding import PartitionSpec as P

first_decay = 0.9
second_decay = 0.95
adam_epsilon = 1e-08
ROWS = 16
COLS = 512
PARTS = 1
LANES = 128
GRADS = 12
OUTPUTS = 16
VMEM_BYTES = 52 * 1024 * 1024


def dot(a, b, contract_a, contract_b):
    return lax.dot_general(
        a, b, (((contract_a,), (contract_b,)), ((), ())), preferred_element_type=jnp.float32
    )


def kernel(
    places,
    n_hidden,
    capacity,
    swap_ref,
    ids_ref,
    route_ref,
    acts_ref,
    gout_ref,
    w_hbm,
    m_hbm,
    v_hbm,
    comb_ref,
    ggu_ref,
    upd_hbm,
    w_all,
    m_here,
    v_here,
    table,
    h_send,
    h_recv,
    g_send,
    g_recv,
    g_rows,
    w_recv,
    h_own,
    h_all,
    y_send,
    y_recv,
    y_rows,
    gw_send,
    gw_recv,
    gh_send,
    gh_recv,
    gr_send,
    gr_recv,
    u_here,
    u_mid,
    u_out,
    partner_row,
    partner_ref,
    local_sem,
    send_sem,
    recv_sem,
):
    me = lax.axis_index("expert")
    mine = lax.axis_index("hidden")
    tok = ids_ref.shape[1]
    count = 2 * tok
    slots = places * capacity
    unit = h_own.shape[1]
    feat = gout_ref.shape[0]
    row_groups = m_here.shape[0] // ROWS
    col_groups = m_here.shape[1] // COLS
    stride = places // row_groups
    halves = 2 if row_groups % 2 == 0 else 1
    half_rows = m_here.shape[0] // halves

    def far_first(at, step, length):
        near = length - step
        half = (near + 1) // 2
        return lax.rem(at + half + (1 - lax.rem(near, 2)) * (length - 2 * half), length)

    def expert_peer(step):
        return far_first(me, step, places)

    def hidden_peer(step):
        return lax.rem(mine + step, n_hidden)

    barrier = pltpu.get_barrier_semaphore()

    def greet_expert(step, carry):
        pl.semaphore_signal(barrier, inc=1, device_id={"expert": expert_peer(step)})
        return carry

    def greet_hidden(step, carry):
        pl.semaphore_signal(barrier, inc=1, device_id={"hidden": hidden_peer(step)})
        return carry

    lax.fori_loop(1, places, greet_expert, 0)
    lax.fori_loop(1, n_hidden, greet_hidden, 0)

    loads = [
        pltpu.make_async_copy(src, dst, local_sem.at[at])
        for at, (src, dst) in enumerate(((m_hbm, m_here), (v_hbm, v_here)))
    ]
    for load in loads:
        load.start()

    ids = jnp.concatenate([ids_ref[0:1, :], ids_ref[1:2, :]], axis=1)
    hot = (lax.broadcasted_iota(jnp.int32, (places, count), 0) == ids).astype(jnp.float32)
    earlier = (
        lax.broadcasted_iota(jnp.int32, (count, count), 0)
        < lax.broadcasted_iota(jnp.int32, (count, count), 1)
    ).astype(jnp.bfloat16)
    before = dot(hot.astype(jnp.bfloat16), earlier, 1, 0)
    rank = jnp.sum(before * hot, axis=0, keepdims=True).astype(jnp.int32)
    slot = ids * capacity + rank
    table[...] = (lax.broadcasted_iota(jnp.int32, (slots, count), 0) == slot).astype(jnp.bfloat16)

    def gate_and_up(choice):
        at = choice * 2 * unit
        gate = acts_ref[:, at : at + unit].astype(jnp.float32)
        up = acts_ref[:, at + unit : at + 2 * unit].astype(jnp.float32)
        return gate, up

    rows = []
    for choice in range(2):
        gate, up = gate_and_up(choice)
        rows.append((gate * jax.nn.sigmoid(gate) * up).astype(jnp.bfloat16))
    placed = dot(table[...], jnp.concatenate(rows, axis=0), 1, 0)
    h_send[...] = placed.reshape(places, capacity, unit).astype(jnp.bfloat16)

    unsent = []

    def arrived(dst, at):
        pltpu.make_async_copy(dst, dst, recv_sem.at[at]).wait()

    def sent(src, at):
        pltpu.make_async_copy(src, src, send_sem.at[at]).wait()

    def to_experts(src, dst, at):
        def send(step, carry):
            peer = expert_peer(step)
            pltpu.make_async_remote_copy(
                src_ref=src.at[peer],
                dst_ref=dst.at[me],
                send_sem=send_sem.at[at],
                recv_sem=recv_sem.at[at],
                device_id={"expert": peer},
            ).start()
            return carry

        lax.fori_loop(1, places, send, 0)
        pltpu.make_async_copy(src.at[me], dst.at[me], recv_sem.at[at]).start()
        unsent.append((dst.at[pl.ds(0, places - 1)], at))

    def to_hidden(pick, dst, at):
        def send(step, carry):
            peer = hidden_peer(step)
            pltpu.make_async_remote_copy(
                src_ref=pick(peer),
                dst_ref=dst.at[mine],
                send_sem=send_sem.at[at],
                recv_sem=recv_sem.at[at],
                device_id={"hidden": peer},
            ).start()
            return carry

        lax.fori_loop(1, n_hidden, send, 0)
        pltpu.make_async_copy(pick(mine), dst.at[mine], recv_sem.at[at]).start()
        unsent.append((dst.at[pl.ds(0, n_hidden - 1)], at))

    rows = [
        (route_ref[choice : choice + 1, :] * gout_ref[...].astype(jnp.float32)).astype(jnp.bfloat16)
        for choice in range(2)
    ]
    placed = dot(table[...], jnp.concatenate(rows, axis=1), 1, 1)
    core = lax.rem(me, 2)
    span = g_recv.shape[2]
    rest = 2 * feat - span

    def paired(rows):
        rows = rows.reshape(places // 2, 2, capacity, feat)
        return jnp.concatenate([rows[:, 0], rows[:, 1]], axis=2).astype(jnp.bfloat16)

    def to_chips(src, dst, at, first=1, last=places // 2):
        def to_core(chip, side):
            if side == 0:
                part, target = src.at[chip, :, pl.ds(0, span)], dst.at[me]
            else:
                part, target = src.at[chip, :, pl.ds(span, rest)], dst.at[me, :, pl.ds(span - rest, rest)]
            return part, target

        def start(chip, side):
            part, target = to_core(chip, side)
            pltpu.make_async_remote_copy(
                src_ref=part,
                dst_ref=target,
                send_sem=send_sem.at[at + side],
                recv_sem=recv_sem.at[at],
                device_id={"expert": 2 * chip + side},
            ).start()

        def send(step, carry):
            chip = far_first(me // 2, step, places // 2)
            start(chip, 0)
            start(chip, 1)
            return carry

        lax.fori_loop(first, last, send, 0)
        if last == places // 2:
            for side in range(2):

                @pl.when(core == side)
                def _(side=side):
                    start(me // 2, 1 - side)
                    part, target = to_core(me // 2, side)
                    pltpu.make_async_copy(part, target, recv_sem.at[at]).start()

    def from_chips(dst, rows, at):
        def unpack(offset):
            return dst[:, :, offset : offset + feat].astype(jnp.float32).reshape(slots, feat).astype(jnp.bfloat16)

        seam = dst.at[:, :, pl.ds(span - LANES, LANES)]
        other = dst.at[:, :, pl.ds(0, LANES)]

        @pl.when(core == 0)
        def _():
            arrived(dst, at)
            if rest < span:
                pltpu.make_async_remote_copy(
                    src_ref=seam,
                    dst_ref=other,
                    send_sem=send_sem.at[at + 2],
                    recv_sem=recv_sem.at[at + 1],
                    device_id={"expert": me + 1},
                ).start()
            rows[...] = unpack(0)

        @pl.when(core == 1)
        def _():
            arrived(dst.at[:, :, pl.ds(span - rest, rest)], at)
            if rest < span:
                arrived(other, at + 1)
            rows[...] = unpack(span - feat)

    def chips_sent(dst, at):
        half = places // 2
        for side in range(2):

            @pl.when(core == side)
            def _(side=side):
                sent(dst.at[pl.ds(0, half - (side == 0))], at)
                sent(dst.at[pl.ds(0, half - (side == 1)), :, pl.ds(0, rest)], at + 1)

        if rest < span:

            @pl.when(core == 0)
            def _():
                sent(dst.at[:, :, pl.ds(0, LANES)], at + 2)

    g_send[...] = paired(placed)
    def send_blocks(product, src, dst, at):
        def send(step, carry):
            peer = hidden_peer(step)
            src[peer] = product(peer).astype(jnp.bfloat16)
            pltpu.make_async_remote_copy(
                src_ref=src.at[peer],
                dst_ref=dst.at[mine],
                send_sem=send_sem.at[at],
                recv_sem=recv_sem.at[at],
                device_id={"hidden": peer},
            ).start()
            return carry

        lax.fori_loop(1, n_hidden, send, 0)
        src[mine] = product(mine).astype(jnp.bfloat16)
        pltpu.make_async_copy(src.at[mine], dst.at[mine], recv_sem.at[at]).start()
        unsent.append((dst.at[pl.ds(0, n_hidden - 1)], at))

    pl.semaphore_wait(barrier, places + n_hidden - 2)
    def weight_window(peer):
        at = pl.multiple_of(peer * feat // LANES * LANES, LANES)
        return w_hbm.at[:, pl.ds(at, span)]

    to_hidden(weight_window, w_recv, 1)
    to_experts(h_send, h_recv, 0)
    to_chips(g_send, g_recv, GRADS)

    place = lax.broadcasted_iota(jnp.int32, (128, swap_ref.shape[1]), 0)
    left, right = swap_ref[0:1, :], swap_ref[1:2, :]
    trades = jnp.where(place == left, right, 0) + jnp.where(place == right, left, 0)
    trades = jnp.sum(trades, axis=1, keepdims=True)
    partner_row[...] = jnp.broadcast_to(trades, (128, 128)).T[0:1, :]
    table_copy = pltpu.make_async_copy(partner_row, partner_ref, local_sem.at[3])
    table_copy.start()

    arrived(h_recv, 0)
    h_own[...] = h_recv[...].astype(jnp.float32).reshape(slots, unit).astype(jnp.bfloat16)
    to_hidden(lambda peer: h_own, h_all, 3)
    arrived(w_recv, 1)
    shift = span - feat

    @pl.when(lax.rem(mine * feat, LANES) == 0)
    def _():
        w_all[...] = w_recv[:, :, :feat]

    @pl.when(lax.rem(mine * feat, LANES) != 0)
    def _():
        w_all[...] = w_recv[:, :, shift:]

    arrived(h_all, 3)
    h_cat = jnp.concatenate([h_all[block] for block in range(n_hidden)], axis=1)
    y_send[...] = paired(dot(h_cat, w_all[...].reshape(n_hidden * unit, feat), 1, 0))
    to_chips(y_send, y_recv, OUTPUTS, 1, places // 4)
    from_chips(g_recv, g_rows, GRADS)
    grads = g_rows[...]
    for half in range(halves):
        part = pl.ds(half * half_rows, half_rows)

        def send_half(step, carry, half=half, part=part):
            peer = hidden_peer(step)
            if half == 0:
                gw_send[peer] = dot(h_all[peer], grads, 0, 0).astype(jnp.bfloat16)
            pltpu.make_async_remote_copy(
                src_ref=gw_send.at[peer, part],
                dst_ref=gw_recv.at[mine, part],
                send_sem=send_sem.at[10 + half],
                recv_sem=recv_sem.at[10 + half],
                device_id={"hidden": peer},
            ).start()
            return carry

        lax.fori_loop(1, n_hidden, send_half, 0)
        if half == 0:
            gw_send[mine] = dot(h_all[mine], grads, 0, 0).astype(jnp.bfloat16)
        pltpu.make_async_copy(
            gw_send.at[mine, part], gw_recv.at[mine, part], recv_sem.at[10 + half]
        ).start()
        unsent.append((gw_recv.at[pl.ds(0, n_hidden - 1), part], 10 + half))
    to_chips(y_send, y_recv, OUTPUTS, places // 4, places // 2)

    for load in loads:
        load.wait()

    def spare_seat(group):
        return stride - 1 - 2 * lax.rem(group, stride // 2)

    def past_spare(at, group):
        return (at + stride - spare_seat(group)) // stride

    my_group, my_seat = me // stride, lax.rem(me, stride)
    is_mid = my_seat != spare_seat(my_group)

    def rows_of(group):
        per_half = row_groups // halves
        seat = lax.rem(group, halves) * per_half + group // halves
        return pl.multiple_of(seat * ROWS, ROWS)

    my_row = rows_of(my_group)
    my_col = (my_seat - past_spare(my_seat, my_group)) * COLS
    wide = COLS // PARTS

    def column_at(base, part):
        return pl.ds(pl.multiple_of(base + part * wide, wide), wide)

    def send_rows(group, part):
        at = rows_of(group)

        def send(col, carry):
            peer = group * stride + col + past_spare(col, group)
            chunk = u_here.at[pl.ds(at, ROWS), column_at(col * COLS, part)]

            @pl.when(peer == me)
            def _():
                pltpu.make_async_copy(chunk, u_mid.at[part, me], recv_sem.at[8 + part]).start()

            @pl.when(peer != me)
            def _():
                pltpu.make_async_remote_copy(
                    src_ref=chunk,
                    dst_ref=u_mid.at[part, me],
                    send_sem=send_sem.at[8 + part],
                    recv_sem=recv_sem.at[8 + part],
                    device_id={"expert": peer},
                ).start()

            return carry

        lax.fori_loop(0, col_groups, send, 0)

    def update_rows(step, carry, half):
        group = halves * far_first(my_group // halves, step, row_groups // halves) + half
        at = rows_of(group)
        for pair in range(n_hidden // 2):
            span = slice(pair * 2 * feat, (pair + 1) * 2 * feat)
            grad = jnp.concatenate(
                [
                    gw_recv[2 * pair, pl.ds(at, ROWS), :],
                    gw_recv[2 * pair + 1, pl.ds(at, ROWS), :],
                ],
                axis=1,
            ).astype(jnp.float32)
            first = m_here[pl.ds(at, ROWS), span].astype(jnp.float32)
            second = v_here[pl.ds(at, ROWS), span].astype(jnp.float32)
            first_new = first_decay * first + (1.0 - first_decay) * grad
            second_new = second_decay * second + (1.0 - second_decay) * grad * grad
            u_here[pl.ds(at, ROWS), span] = (
                first_new / (jnp.sqrt(second_new) + adam_epsilon)
            ).astype(jnp.bfloat16)
        send_rows(group, 0)
        return carry

    for half in range(halves):
        arrived(gw_recv.at[:, pl.ds(half * half_rows, half_rows)], 10 + half)
        lax.fori_loop(
            1, row_groups // halves + 1, functools.partial(update_rows, half=half), 0
        )
    send_blocks(lambda block: dot(grads, w_all[block], 1, 1), gh_send, gh_recv, 6)

    from_chips(y_recv, y_rows, OUTPUTS)
    back = y_rows[...]
    picked = dot(back, table[...], 0, 0)
    comb_ref[...] = (
        route_ref[0:1, :] * picked[:, :tok] + route_ref[1:2, :] * picked[:, tok:]
    ).astype(jnp.bfloat16)
    arrived(gh_recv, 6)
    total = gh_recv[0].astype(jnp.float32)
    for block in range(1, n_hidden):
        total = total + gh_recv[block].astype(jnp.float32)
    gr_send[...] = total.reshape(places, capacity, unit).astype(jnp.bfloat16)

    @pl.when(is_mid)
    def _():
        for part in range(PARTS):
            sent(u_mid.at[part, pl.ds(0, row_groups * col_groups - 1)], 8 + part)

    @pl.when(jnp.logical_not(is_mid))
    def _():
        for part in range(PARTS):
            sent(u_mid.at[part, pl.ds(0, row_groups * col_groups)], 8 + part)

    to_experts(gr_send, gr_recv, 7)
    table_copy.wait()

    @pl.when(is_mid)
    def _():
        for part in range(PARTS):
            arrived(u_mid.at[part], 8 + part)
            target = upd_hbm.at[pl.ds(my_row, ROWS), column_at(my_col, part)]

            def forward(step, carry, part=part, target=target):
                peer = expert_peer(step)
                u_out[part, peer] = u_mid[part, partner_ref[0, peer]]
                pltpu.make_async_remote_copy(
                    src_ref=u_out.at[part, peer],
                    dst_ref=target,
                    send_sem=send_sem.at[8 + PARTS],
                    recv_sem=recv_sem.at[8 + PARTS],
                    device_id={"expert": peer},
                ).start()
                return carry

            lax.fori_loop(1, places, forward, 0)
            u_out[part, me] = u_mid[part, partner_ref[0, me]]
            pltpu.make_async_copy(u_out.at[part, me], target, recv_sem.at[8 + PARTS]).start()

    arrived(gr_recv, 7)
    back = gr_recv[...].astype(jnp.float32).reshape(slots, unit).astype(jnp.bfloat16)
    picked = dot(table[...], back, 0, 0)
    row = lax.broadcasted_iota(jnp.int32, (count, 2 * count), 0)
    column = lax.broadcasted_iota(jnp.int32, (count, 2 * count), 1)
    wanted = 4 * lax.rem(row, tok) + 2 * (row // tok)
    rows = [[], []]
    for choice in range(2):
        gate, up = gate_and_up(choice)
        sig = jax.nn.sigmoid(gate)
        grad_hidden = picked[choice * tok : (choice + 1) * tok]
        rows[0].append(
            (grad_hidden * up * sig * (1.0 + gate * (1.0 - sig))).astype(jnp.bfloat16)
        )
        rows[1].append((grad_hidden * (gate * sig)).astype(jnp.bfloat16))
    spread = [
        dot((column == wanted + kind).astype(jnp.bfloat16), jnp.concatenate(rows[kind], axis=0), 0, 0)
        for kind in range(2)
    ]
    ggu_ref[...] = (spread[0] + spread[1]).astype(jnp.bfloat16)
    for src, at in unsent:
        sent(src, at)
    chips_sent(g_recv, GRADS)
    chips_sent(y_recv, OUTPUTS)

    arrived(upd_hbm, 8 + PARTS)

    @pl.when(is_mid)
    def _():
        for part in range(PARTS):
            sent(u_out.at[part, pl.ds(0, places - 1)], 8 + PARTS)


def hand_out(*refs):
    sources, targets, sem = refs[:3], refs[3:6], refs[6]
    copies = [
        pltpu.make_async_copy(sources[at], targets[at], sem.at[at]) for at in (2, 0, 1)
    ]
    for copy in copies:
        copy.start()
    for copy in copies:
        copy.wait()


def local(
    swap_pairs,
    expert_ids,
    route_weights,
    gate_up,
    grad_out,
    down_weight,
    first_moment,
    second_moment,
):
    places = lax.axis_size("expert")
    n_hidden = lax.axis_size("hidden")
    tok, top = expert_ids.shape
    unit, depth = down_weight.shape[1:]
    feat = grad_out.shape[1]
    capacity = 2 * tok * top // places
    slots = places * capacity
    bf16 = jnp.bfloat16
    vmem = pl.BlockSpec(memory_space=pltpu.VMEM)
    anywhere = pl.BlockSpec(memory_space=pl.ANY)
    scratch = [
        ((n_hidden, unit, feat), bf16),
        ((unit, depth), bf16),
        ((unit, depth), bf16),
        ((slots, tok * top), bf16),
        ((places, capacity, unit), bf16),
        ((places, capacity, unit), bf16),
        ((places // 2, capacity, 2 * feat), bf16),
        ((places, capacity, -(-feat // LANES) * LANES), bf16),
        ((slots, feat), bf16),
        ((n_hidden, unit, -(-feat // LANES) * LANES), bf16),
        ((slots, unit), bf16),
        ((n_hidden, slots, unit), bf16),
        ((places // 2, capacity, 2 * feat), bf16),
        ((places, capacity, -(-feat // LANES) * LANES), bf16),
        ((slots, feat), bf16),
        ((n_hidden, unit, feat), bf16),
        ((n_hidden, unit, feat), bf16),
        ((n_hidden, slots, unit), bf16),
        ((n_hidden, slots, unit), bf16),
        ((places, capacity, unit), bf16),
        ((places, capacity, unit), bf16),
        ((unit, depth), bf16),
        ((PARTS, places, ROWS, COLS // PARTS), bf16),
        ((PARTS, places, ROWS, COLS // PARTS), bf16),
        ((1, 128), jnp.int32),
    ]
    combined, grads, update = pl.pallas_call(
        functools.partial(kernel, places, n_hidden, capacity),
        out_shape=(
            jax.ShapeDtypeStruct((feat, tok), bf16),
            jax.ShapeDtypeStruct((tok * top * 2, unit), bf16),
            jax.ShapeDtypeStruct((unit, depth), bf16),
        ),
        in_specs=[vmem] * 5 + [anywhere] * 3,
        out_specs=(vmem, vmem, anywhere),
        scratch_shapes=[pltpu.VMEM(shape, kind) for shape, kind in scratch]
        + [
            pltpu.SMEM((1, 128), jnp.int32),
            pltpu.SemaphoreType.DMA((4,)),
            pltpu.SemaphoreType.DMA((20,)),
            pltpu.SemaphoreType.DMA((20,)),
        ],
        compiler_params=pltpu.CompilerParams(
            collective_id=0, has_side_effects=True, vmem_limit_bytes=VMEM_BYTES
        ),
    )(
        swap_pairs.T,
        expert_ids.T,
        route_weights.T,
        gate_up.reshape(tok, top * 2 * unit),
        grad_out.T,
        down_weight[0],
        first_moment[0],
        second_moment[0],
    )
    results = (combined, grads, update)
    combined, grads, update = pl.pallas_call(
        hand_out,
        out_shape=tuple(jax.ShapeDtypeStruct(out.shape, out.dtype) for out in results),
        in_specs=[anywhere] * 3,
        out_specs=(anywhere,) * 3,
        scratch_shapes=[pltpu.SemaphoreType.DMA((3,))],
        compiler_params=pltpu.CompilerParams(vmem_limit_bytes=VMEM_BYTES),
    )(*results)
    return combined.T, grads.reshape(tok, top, 2, unit), update[None]


def solution(mesh):
    placed = (
        P(),
        P("expert", None),
        P("expert", None),
        P("expert", None, None, "hidden"),
        P("expert", "hidden"),
        P("expert", "hidden", None),
        P("expert", "hidden", None),
        P("expert", "hidden", None),
    )
    return jax.shard_map(
        local,
        mesh=mesh,
        in_specs=placed,
        out_specs=(
            P("expert", "hidden"),
            P("expert", None, None, "hidden"),
            P("expert", "hidden", None),
        ),
        check_vma=False,
    )
```
